256 devices in a mesh: tensor: 4 (over z_lo, core), request: 64 (over x, y, z_hi).
Axes of the slice: x: 4, y: 4, z: 8 (z_hi: 4, z_lo: 2; z = z_hi * 2 + z_lo), core: 2. Of those that a mesh axis runs over, the one named last changes fastest.
Arguments:
- hidden_in: bfloat16 [16384, 2048], P('request'), may hold values from -6 to 6
- span_q: bfloat16 [16384, 2048], P('request', 'tensor'), may hold values from -170 to 170
- span_k: bfloat16 [16384, 2048], P('request', 'tensor'), may hold values from -7 to 7
- span_v: bfloat16 [16384, 2048], P('request', 'tensor'), may hold values from -6 to 6
- cache_k: bfloat16 [64, 768, 2048], P('request', None, 'tensor'), may hold values from -6 to 6
- cache_v: bfloat16 [64, 768, 2048], P('request', None, 'tensor'), may hold values from -6 to 6
- cached_len: int32 [64], P('request'), may hold values from 0 to 768
- out_proj: bfloat16 [2048, 2048], P('tensor'), may hold values from -0.125 to 0.125
- norm_gain: float32 [2048], replicated, may hold values from 0.1 to 1.9
- routes: int32 [16384, 4], P('request'), may hold values from 0 to 63, all different within a row; in each aligned block of 256 rows (0 to 255, 256 to 511, ...) at most 32 rows name the same one
- route_weight: float32 [16384, 4], P('request'), may hold values from 0.1 to 1
- w_gate: bfloat16 [64, 2048, 1408], P('request', None, 'tensor'), may hold values from -0.125 to 0.125
- w_up: bfloat16 [64, 2048, 1408], P('request', None, 'tensor'), may hold values from -0.125 to 0.125
- w_down: bfloat16 [64, 1408, 2048], P('request', 'tensor'), may hold values from -0.15625 to 0.15625
Outputs:
- layer_out: bfloat16 [16384, 2048], P('request', 'tensor')
- decode_kv: bfloat16 [64, 2, 1024, 2048], P('request', None, 'tensor')
The draws below stay inside these ranges and needn't reach their ends.
Inputs may be any that keep to these rules, and one draw needn't show every extreme that they name: `routes`: among the rows of one request no expert is named more than 32 times.
All inputs are finite; a program needn't handle non-finite values.
Results may differ from the reference program's by a relative error of at most 0.014.
Values may be sent and summed in bfloat16 or wider, within the bound.
No kernel may reach another device: no remote copies, remote signals or barrier semaphores. Data moves between devices by JAX's collectives and lax.ppermute only.
A program may use at most 128 MiB of HBM per device.

```python
import math
import jax
import jax.numpy as jnp
import numpy as np
from jax import lax

D = 2048
HEADS = 16
HD = 128
EXPERT_FF = 1408
TOP = 4
SPAN = 256
PRIOR = 768
REQS = 64
EXPERTS = 64
TOKENS = 16384
CTX = 1024
MOST = 32
N_TENSOR = 4


def span_pair(key):
    base = jax.random.fold_in(key, 101)
    keys = jnp.clip(jax.random.normal(jax.random.fold_in(base, 1), (TOKENS, HEADS * HD), jnp.float32), -6.0, 6.0)
    queries = jnp.clip(jax.random.normal(jax.random.fold_in(base, 2), (TOKENS, HEADS * HD), jnp.float32), -6.0, 6.0)
    return (queries, keys)


def draw_span_q(key, part):
    queries, keys = span_pair(key)
    return queries.astype(jnp.bfloat16)


def draw_span_k(key, part):
    queries, keys = span_pair(key)
    return keys.astype(jnp.bfloat16)


def draw_cached_len(key, part):
    lengths = jax.random.randint(jax.random.fold_in(key, 7), (REQS,), 0, PRIOR + 1)
    longest = jax.random.randint(jax.random.fold_in(key, 8), (), 0, REQS)
    return jnp.where(jnp.arange(REQS) == longest, PRIOR, lengths).astype(jnp.int32)


def block_levels(own_key, extent, split, least, top_value):
    level, own = 1.0, jax.random.fold_in(own_key, 6)
    for dim, blocks in split:
        draws = jnp.exp(jax.random.uniform(jax.random.fold_in(own, dim), (blocks,), jnp.float32, least / len(split), top_value / len(split)))
        level = level * jnp.repeat(draws, extent[dim] // blocks).reshape([-1 if axis == dim else 1 for axis in range(len(extent))])
    return level


def routed_block(stream_key, own, number, rows, number_of, top, bound, slope):
    ranking = jax.random.permutation(stream_key, number_of)
    crowded, usual = portions_of(number_of, rows * top, bound, slope, True), portions_of(number_of, rows * top, bound, slope, False)
    places = jnp.arange(number_of)

    def named(sizes, turn):
        used = int((sizes > 0).sum())
        fixed = max(1, used // 4)
        moved = fixed + (places - fixed + turn * (used - fixed)) % max(1, number_of - fixed)
        return jnp.zeros((number_of,), jnp.int32).at[ranking[jnp.where(places < fixed, places, moved)]].set(jnp.asarray(sizes, jnp.int32))

    sizes = jnp.where(number % 4 == 0, named(crowded, number // 4), named(usual, number - number // 4 - 1))
    mixed = jax.random.permutation(jax.random.fold_in(own, 3), number_of)
    giver, receiver = mixed[0:number_of // 2 * 2:2], mixed[1:number_of // 2 * 2:2]
    room = jnp.minimum(sizes[giver] - 1, bound - sizes[receiver]) // 2
    room = jnp.where((giver == ranking[0]) | (receiver == ranking[0]) | (sizes[receiver] == 0), 0, jnp.maximum(room, 0))
    moved = jax.random.randint(jax.random.fold_in(own, 4), (number_of // 2,), 0, 1 << 20) % (room + 1)
    sizes = sizes.at[giver].add(-moved).at[receiver].add(moved)
    members = jnp.searchsorted(jnp.cumsum(sizes), jnp.arange(rows * top), side="right").astype(jnp.int32)
    grid = members.reshape(top, rows).T
    grid = grid[jax.random.permutation(jax.random.fold_in(own, 1), rows)]
    turn = jax.random.randint(jax.random.fold_in(own, 2), (rows, 1), 0, top)
    return jnp.take_along_axis(grid, (jnp.arange(top)[None, :] + turn) % top, axis=1)


def portions_of(count, total, limit, skew, full):
    loads = [(1 << 20) // math.isqrt(rank ** skew) + 1 for rank in range(1, count + 1)]
    largest = limit if full else min(limit, max(-(-total // count), total * loads[0] // sum(loads)))
    least = 1 if total - largest >= count - 1 else 0
    holding, spare = [largest] + [least] * (count - 1), total - largest - least * (count - 1)
    while spare > 0:
        movable = [i for i in range(1, count) if holding[i] < largest] or [i for i in range(1, count) if holding[i] < limit]
        mass, budget = sum([loads[i] for i in movable]), spare
        for i in movable:
            addition = min(limit - holding[i], max(1, budget * loads[i] // mass), spare)
            holding[i] = holding[i] + addition
            spare = spare - addition
    return np.array(holding)


def scatter_about(rng, extent, scale, reach, cuts=(), kind=jnp.bfloat16):
    factor_of = block_levels(rng, extent, cuts, -0.22, 0.18) if cuts else 1.0
    values = jax.random.normal(rng, extent, jnp.float32) * scale * factor_of
    return jnp.minimum(jnp.maximum(values, -reach), reach).astype(kind)


def setup_inputs(seed: int = 0) -> dict:
    streams_of = jax.random.split(jax.random.key(seed), 15)
    hidden_in = scatter_about(streams_of[0], (TOKENS, D), 1.0, 6.0, ((0, 64),))
    span_q = draw_span_q(jax.random.fold_in(streams_of[14], 71), 0)
    span_k = draw_span_k(jax.random.fold_in(streams_of[14], 71), 0)
    span_v = scatter_about(streams_of[3], (TOKENS, HEADS * HD), 1.0, 6.0, ((0, 64), (1, 4)))
    cache_k = scatter_about(streams_of[4], (REQS, PRIOR, HEADS * HD), 1.0, 6.0, ((0, 64), (2, 4)))
    cache_v = scatter_about(streams_of[5], (REQS, PRIOR, HEADS * HD), 1.0, 6.0, ((0, 64), (2, 4)))
    cached_len = draw_cached_len(jax.random.fold_in(streams_of[14], 71), 0)
    out_proj = scatter_about(streams_of[7], (HEADS * HD, D), (HEADS * HD) ** -0.5, 0.125, ((0, 4),))
    norm_gain = jnp.clip(1.0 + 0.18 * jax.random.normal(streams_of[8], (D,), jnp.float32), 0.1, 1.9)
    routes_keys = jax.random.split(jax.random.fold_in(streams_of[9], 1), TOKENS // SPAN)
    routes_turns = jax.random.permutation(jax.random.fold_in(streams_of[9], 3), TOKENS // SPAN)
    routes = jax.vmap(lambda own, number: routed_block(jax.random.fold_in(streams_of[9], 2), own, number, SPAN, EXPERTS, TOP, MOST, 2))(routes_keys, routes_turns).reshape((TOKENS, TOP))
    route_weight = jnp.clip(jnp.exp(math.log(1.0) - 2.3025851 * jax.random.uniform(streams_of[10], (TOKENS, TOP), jnp.float32) ** block_levels(streams_of[10], (TOKENS, TOP), ((0, 64),), -0.2, 0.2)), 0.1, 1.0)
    w_gate = scatter_about(streams_of[11], (EXPERTS, D, EXPERT_FF), D ** -0.5, 0.125, ((0, 64), (2, 4)))
    w_up = scatter_about(streams_of[12], (EXPERTS, D, EXPERT_FF), D ** -0.5, 0.125, ((0, 64), (2, 4)))
    w_down = scatter_about(streams_of[13], (EXPERTS, EXPERT_FF, D), EXPERT_FF ** -0.5, 0.15625, ((0, 64), (1, 4)))
    return {"hidden_in": hidden_in, "span_q": span_q, "span_k": span_k, "span_v": span_v, "cache_k": cache_k, "cache_v": cache_v, "cached_len": cached_len, "out_proj": out_proj, "norm_gain": norm_gain, "routes": routes, "route_weight": route_weight, "w_gate": w_gate, "w_up": w_up, "w_down": w_down}


eps = 1e-06
neg_large = -1e+30
block_rows = 128

def place(cached, fresh, length):
    positions = jnp.arange(CTX, dtype=jnp.int32)
    padded = jnp.concatenate([cached, jnp.zeros((SPAN, cached.shape[1]), cached.dtype)], axis=0)
    kept = jnp.where((positions < length)[:, None], padded, jnp.zeros_like(padded))
    return lax.dynamic_update_slice(kept, fresh, (length.astype(jnp.int32), jnp.int32(0)))

def reference(hidden_in, span_q, span_k, span_v, cache_k, cache_v, cached_len, out_proj, norm_gain, routes, route_weight, w_gate, w_up, w_down):

    def one_request(index):
        start = (index * SPAN).astype(jnp.int32)
        query = lax.dynamic_slice_in_dim(span_q, start, SPAN, 0)
        new_keys = lax.dynamic_slice_in_dim(span_k, start, SPAN, 0)
        new_values = lax.dynamic_slice_in_dim(span_v, start, SPAN, 0)
        old_keys = lax.dynamic_index_in_dim(cache_k, index, 0, keepdims=False)
        old_values = lax.dynamic_index_in_dim(cache_v, index, 0, keepdims=False)
        length = lax.dynamic_index_in_dim(cached_len, index, 0, keepdims=False)
        keys = jnp.concatenate([old_keys, new_keys], axis=0).reshape(CTX, HEADS, HD)
        values = jnp.concatenate([old_values, new_values], axis=0).reshape(CTX, HEADS, HD)
        scores = jnp.einsum('qhd,khd->hqk', query.reshape(SPAN, HEADS, HD).astype(jnp.float32), keys.astype(jnp.float32)) * HD ** (-0.5)
        key_pos = jnp.arange(CTX, dtype=jnp.int32)[None, :]
        row_pos = jnp.arange(SPAN, dtype=jnp.int32)[:, None]
        valid = jnp.where(key_pos < PRIOR, key_pos < length, key_pos - PRIOR <= row_pos)
        scores = jnp.where(valid[None], scores, neg_large)
        top = lax.optimization_barrier(jnp.max(scores, axis=2, keepdims=True))
        weights = jnp.exp(scores - top)
        probs = (weights / lax.optimization_barrier(jnp.sum(weights, axis=2, keepdims=True))).astype(jnp.bfloat16)
        attended = jnp.einsum('hqk,khd->qhd', probs.astype(jnp.float32), values.astype(jnp.float32)).astype(jnp.bfloat16)
        decode = jnp.stack([place(old_keys, new_keys, length), place(old_values, new_values, length)], axis=0)
        return (attended.reshape(SPAN, HEADS * HD), decode)
    attended, decode_kv = lax.map(one_request, jnp.arange(REQS, dtype=jnp.int32))
    attended = attended.reshape(TOKENS, HEADS * HD)
    mixed = (hidden_in.astype(jnp.float32) + jnp.dot(attended, out_proj, preferred_element_type=jnp.float32)).astype(jnp.bfloat16)
    mixed_f = mixed.astype(jnp.float32)
    normed = (mixed_f * lax.rsqrt(lax.optimization_barrier(jnp.mean(mixed_f * mixed_f, axis=1, keepdims=True)) + eps) * norm_gain).astype(jnp.bfloat16)
    total = TOKENS * TOP
    flat = routes.reshape(-1).astype(jnp.int32)
    onehot = (flat[:, None] == jnp.arange(EXPERTS, dtype=jnp.int32)[None, :]).astype(jnp.int32)
    before = jnp.cumsum(onehot, axis=0) - onehot
    rank = lax.optimization_barrier(jnp.sum(before * onehot, axis=1))
    counts = lax.optimization_barrier(jnp.sum(onehot, axis=0))
    padded_counts = (counts + block_rows - 1) // block_rows * block_rows
    ends = jnp.cumsum(padded_counts)
    starts = ends - padded_counts
    position = starts[flat] + rank
    pad_rows = total + EXPERTS * block_rows
    blocks = pad_rows // block_rows
    source_row = jnp.arange(total, dtype=jnp.int32) // TOP
    buffer = jnp.zeros((pad_rows, D), jnp.bfloat16).at[position].set(normed[source_row])
    block_start = jnp.arange(blocks, dtype=jnp.int32) * block_rows
    block_expert = jnp.minimum(lax.optimization_barrier(jnp.sum((ends[None, :] <= block_start[:, None]).astype(jnp.int32), axis=1)), EXPERTS - 1)
    slice_ff = EXPERT_FF // N_TENSOR

    def expert_block(pair):
        rows, expert = pair
        gate_w = lax.dynamic_index_in_dim(w_gate, expert, 0, keepdims=False)
        up_w = lax.dynamic_index_in_dim(w_up, expert, 0, keepdims=False)
        down_w = lax.dynamic_index_in_dim(w_down, expert, 0, keepdims=False)
        gate = jnp.dot(rows, gate_w, preferred_element_type=jnp.float32)
        upper = jnp.dot(rows, up_w, preferred_element_type=jnp.float32)
        act = (jax.nn.silu(gate) * upper).astype(jnp.bfloat16)
        summed = jnp.zeros((rows.shape[0], D), jnp.float32)
        for piece in range(N_TENSOR):
            part = jnp.dot(act[:, piece * slice_ff:(piece + 1) * slice_ff], down_w[piece * slice_ff:(piece + 1) * slice_ff], preferred_element_type=jnp.float32)
            rounded = lax.optimization_barrier(part.astype(jnp.bfloat16))
            summed = summed + rounded.astype(jnp.float32)
        return summed.astype(jnp.bfloat16)
    results = lax.map(expert_block, (buffer.reshape(blocks, block_rows, D), block_expert))
    expert_out = results.reshape(pad_rows, D)[position].reshape(TOKENS, TOP, D)
    mixture = lax.optimization_barrier(jnp.sum(expert_out.astype(jnp.float32) * route_weight[:, :, None], axis=1))
    layer_out = (mixed_f + mixture).astype(jnp.bfloat16)
    return (layer_out, decode_kv)
```

```python
import jax
import jax.numpy as jnp
from jax import lax
from jax.sharding import PartitionSpec as P


HD = 128
TOP = 4


eps = 1e-06
neg_large = -1e30


def attend(span_q, span_k, span_v, cache_k, cache_v, length):
    span = span_q.shape[0]
    prior = cache_k.shape[1]
    heads = span_q.shape[1] // HD
    keys = jnp.concatenate([cache_k[0], span_k], axis=0).reshape(prior + span, heads, HD)
    values = jnp.concatenate([cache_v[0], span_v], axis=0).reshape(prior + span, heads, HD)
    query = span_q.reshape(span, heads, HD)
    scores = lax.dot_general(
        query, keys, (((2,), (2,)), ((1,), (1,))), preferred_element_type=jnp.float32
    )
    scores = scores * HD ** (-0.5)
    key_pos = jnp.arange(prior + span, dtype=jnp.int32)[None, :]
    row_pos = jnp.arange(span, dtype=jnp.int32)[:, None]
    valid = jnp.where(key_pos < prior, key_pos < length, key_pos - prior <= row_pos)
    scores = jnp.where(valid[None], scores, neg_large)
    top = jnp.max(scores, axis=2, keepdims=True)
    weights = jnp.exp(scores - top)
    probs = (weights / jnp.sum(weights, axis=2, keepdims=True)).astype(jnp.bfloat16)
    attended = jnp.einsum("hqk,khd->qhd", probs, values, preferred_element_type=jnp.float32)
    return attended.astype(jnp.bfloat16).reshape(span, heads * HD)


def place(cached, fresh, length, context):
    span = fresh.shape[0]
    positions = jnp.arange(context, dtype=jnp.int32)
    padded = jnp.concatenate([cached[0], jnp.zeros((span, cached.shape[2]), cached.dtype)], axis=0)
    kept = jnp.where((positions < length)[:, None], padded, jnp.zeros_like(padded))
    return lax.dynamic_update_slice(kept, fresh, (length, jnp.int32(0)))


def flip(value, mask):
    groups = lax.axis_size("tensor")
    return lax.ppermute(value, "tensor", [(i, i ^ mask) for i in range(groups)])


def on_device(
    hidden_in,
    span_q,
    span_k,
    span_v,
    cache_k,
    cache_v,
    cached_len,
    out_proj,
    norm_gain,
    routes,
    route_weight,
    w_gate,
    w_up,
    w_down,
):
    span, width = hidden_in.shape
    groups = lax.axis_size("tensor")
    experts = lax.axis_size("request")
    quarter = width // groups
    half = width // 2
    me = lax.axis_index("tensor")
    core = me % 2
    length = cached_len[0]

    own_w = (w_gate[0], w_up[0], w_down[0])
    far_w, near_w, diag_w = [], [], []
    for shard in own_w:
        far_w.append(flip(shard, 2))
        near_w.append(flip(shard, 1))
        diag_w.append(flip(far_w[-1], 1))

    most = max(2, 2 * span * TOP // experts)
    share = most // groups
    expert_ids = jnp.arange(experts, dtype=jnp.int32)
    hit = routes[:, :, None] == expert_ids[None, None, :]
    member = jnp.any(hit, axis=1)
    weight_of = jnp.sum(jnp.where(hit, route_weight[:, :, None], 0.0), axis=1)
    lower = jnp.arange(span)[:, None] > jnp.arange(span)[None, :]
    rank = jnp.dot(
        lower.astype(jnp.bfloat16), member.astype(jnp.bfloat16), preferred_element_type=jnp.float32
    ).astype(jnp.int32)
    slot = jnp.where(member, rank - me * share, -1)
    chosen = slot[:, :, None] == jnp.arange(share, dtype=jnp.int32)[None, None, :]
    select = chosen.reshape(span, experts * share).astype(jnp.bfloat16)
    w_hi = lax.reduce_precision(weight_of, 8, 7)
    w_lo = weight_of - w_hi
    mix_hi = jnp.where(chosen, w_hi[:, :, None], 0.0).reshape(span, experts * share)
    mix_lo = jnp.where(chosen, w_lo[:, :, None], 0.0).reshape(span, experts * share)
    mix_hi = mix_hi.astype(jnp.bfloat16)
    mix_lo = mix_lo.astype(jnp.bfloat16)

    attended = attend(span_q, span_k, span_v, cache_k, cache_v, length)
    part = jnp.dot(attended, out_proj, preferred_element_type=jnp.float32)
    chip = part + flip(part.astype(jnp.bfloat16), 1).astype(jnp.float32)
    chip_half = lax.dynamic_slice_in_dim(chip, core * half, half, 1)
    full_half = chip_half + flip(chip_half.astype(jnp.bfloat16), 2).astype(jnp.float32)
    hidden_half = lax.dynamic_slice_in_dim(hidden_in, core * half, half, 1)
    mixed_half = (hidden_half.astype(jnp.float32) + full_half).astype(jnp.bfloat16)
    other_half = flip(mixed_half, 1)
    first = core == 0
    mixed = jnp.concatenate(
        [jnp.where(first, mixed_half, other_half), jnp.where(first, other_half, mixed_half)], axis=1
    )
    mixed_f = mixed.astype(jnp.float32)
    normed = (
        mixed_f * lax.rsqrt(jnp.mean(mixed_f * mixed_f, axis=1, keepdims=True) + eps) * norm_gain
    ).astype(jnp.bfloat16)
    own_mixed = lax.dynamic_slice_in_dim(mixed, me * quarter, quarter, 1)

    outbox = lax.dot_general(
        select, normed, (((0,), (0,)), ((), ())), preferred_element_type=jnp.float32
    ).astype(jnp.bfloat16)
    inbox = lax.all_to_all(outbox, "request", split_axis=0, concat_axis=0, tiled=True)

    context = cache_k.shape[1] + span
    local = jnp.stack(
        [place(cache_k, span_k, length, context), place(cache_v, span_v, length, context)], axis=0
    )
    local, inbox = lax.optimization_barrier((local, inbox))

    total = jnp.zeros((inbox.shape[0], width), jnp.float32)
    for gate_w, up_w, down_w in (own_w, near_w, far_w, diag_w):
        gate = jnp.dot(inbox, gate_w, preferred_element_type=jnp.float32)
        upper = jnp.dot(inbox, up_w, preferred_element_type=jnp.float32)
        act = (jax.nn.silu(gate) * upper).astype(jnp.bfloat16)
        total = total + jnp.dot(act, down_w, preferred_element_type=jnp.float32)
    expert_out = total.astype(jnp.bfloat16)

    block = context // groups
    decode = jnp.zeros((2, block, width), jnp.bfloat16)
    for mask in range(groups):
        peer = me ^ mask
        piece = lax.dynamic_slice_in_dim(local, peer * block, block, 1)
        if mask:
            piece = flip(piece, mask)
        decode = lax.dynamic_update_slice_in_dim(decode, piece, peer * quarter, 2)

    returned = lax.all_to_all(expert_out, "request", split_axis=0, concat_axis=0, tiled=True)
    mixture = jnp.dot(mix_hi, returned, preferred_element_type=jnp.float32) + jnp.dot(
        mix_lo, returned, preferred_element_type=jnp.float32
    )
    result = own_mixed.astype(jnp.float32) + lax.dynamic_slice_in_dim(
        mixture, me * quarter, quarter, 1
    )
    for mask in range(1, groups):
        piece = lax.dynamic_slice_in_dim(mixture, (me ^ mask) * quarter, quarter, 1)
        result = result + flip(piece.astype(jnp.bfloat16), mask).astype(jnp.float32)
    layer_out = result.astype(jnp.bfloat16)
    return (layer_out, decode[None])


def solution(mesh):
    in_specs = (
        P("request", None),
        P("request", "tensor"),
        P("request", "tensor"),
        P("request", "tensor"),
        P("request", None, "tensor"),
        P("request", None, "tensor"),
        P("request"),
        P("tensor", None),
        P(),
        P("request", None),
        P("request", None),
        P("request", None, "tensor"),
        P("request", None, "tensor"),
        P("request", "tensor", None),
    )
    out_specs = (P("request", "tensor"), P("request", None, "tensor", None))

    return jax.shard_map(
        on_device, mesh=mesh, in_specs=in_specs, out_specs=out_specs, check_vma=False
    )
```

```python
import jax
import jax.numpy as jnp
from jax import lax
from jax.experimental import pallas as pl
from jax.experimental.pallas import tpu as pltpu
from jax.sharding import PartitionSpec as P


HD = 128
TOP = 4
RING = 4


eps = 1e-06
neg_large = -1e30


NT = (((1,), (1,)), ((), ()))
TN = (((0,), (0,)), ((), ()))
VMEM = pl.BlockSpec(memory_space=pltpu.VMEM)
SMEM = pl.BlockSpec(memory_space=pltpu.SMEM)


def lanes(start, size):
    return pl.ds(pl.multiple_of(start, 128), size)


def attend_kernel(
    scalars_ref, q_ref, k_ref, v_ref, ck_ref, cv_ref, w_ref, keep_ref, send_ref, part_ref
):
    head = pl.program_id(0)
    length, core = scalars_ref[0], scalars_ref[1]
    query = q_ref[...]
    scale = HD ** (-0.5)
    old = lax.dot_general(query, ck_ref[...], NT, preferred_element_type=jnp.float32) * scale
    new = lax.dot_general(query, k_ref[...], NT, preferred_element_type=jnp.float32) * scale
    old = jnp.where(lax.broadcasted_iota(jnp.int32, old.shape, 1) < length, old, neg_large)
    rows = lax.broadcasted_iota(jnp.int32, new.shape, 0)
    new = jnp.where(lax.broadcasted_iota(jnp.int32, new.shape, 1) <= rows, new, neg_large)
    top = jnp.maximum(
        jnp.max(old, axis=1, keepdims=True), jnp.max(new, axis=1, keepdims=True)
    )
    old = jnp.exp(old - top)
    new = jnp.exp(new - top)
    inverse = 1.0 / (jnp.sum(old, axis=1, keepdims=True) + jnp.sum(new, axis=1, keepdims=True))
    attended = jnp.dot(
        (old * inverse).astype(jnp.bfloat16), cv_ref[...], preferred_element_type=jnp.float32
    ) + jnp.dot(
        (new * inverse).astype(jnp.bfloat16), v_ref[...], preferred_element_type=jnp.float32
    )
    part = jnp.dot(
        attended.astype(jnp.bfloat16), w_ref[...], preferred_element_type=jnp.float32
    )

    @pl.when(head == 0)
    def _():
        part_ref[...] = part

    @pl.when(head > 0)
    def _():
        part_ref[...] += part

    @pl.when(head == pl.num_programs(0) - 1)
    def _():
        half = keep_ref.shape[1]
        keep_ref[...] = part_ref[:, lanes(core * half, half)]
        send_ref[...] = part_ref[:, lanes((1 - core) * half, half)].astype(jnp.bfloat16)


def attend(scalars, span_q, span_k, span_v, cache_k, cache_v, out_proj):
    span, columns = span_q.shape
    prior = cache_k.shape[0]
    width = out_proj.shape[1]
    heads = columns // HD
    fresh = pl.BlockSpec((span, HD), lambda h, n: (0, h))
    cached = pl.BlockSpec((prior, HD), lambda h, n: (0, h))
    halves = pl.BlockSpec((span, width // 2), lambda h, n: (0, 0))
    return pl.pallas_call(
        attend_kernel,
        grid_spec=pltpu.PrefetchScalarGridSpec(
            num_scalar_prefetch=1,
            grid=(heads,),
            in_specs=[
                fresh,
                fresh,
                fresh,
                cached,
                cached,
                pl.BlockSpec((HD, width), lambda h, n: (h, 0)),
            ],
            out_specs=[halves, halves],
            scratch_shapes=[pltpu.VMEM((span, width), jnp.float32)],
        ),
        out_shape=[
            jax.ShapeDtypeStruct((span, width // 2), jnp.float32),
            jax.ShapeDtypeStruct((span, width // 2), jnp.bfloat16),
        ],
        cost_estimate=pl.CostEstimate(
            flops=heads * span * (4 * (prior + span) * HD + 2 * HD * width),
            transcendentals=heads * span * (prior + span),
            bytes_accessed=9 << 20,
        ),
        name="attend",
    )(scalars, span_q, span_k, span_v, cache_k, cache_v, out_proj)


def norm_kernel(scalars_ref, mine_ref, other_ref, gain_ref, mine_out, other_out, own_out):
    chip, core = scalars_ref[0], scalars_ref[1]
    half = mine_ref.shape[1]
    quarter = half // 2
    mine = mine_ref[...].astype(jnp.float32)
    other = other_ref[...].astype(jnp.float32)
    total = jnp.sum(mine * mine, axis=1, keepdims=True) + jnp.sum(
        other * other, axis=1, keepdims=True
    )
    scale = lax.rsqrt(total / (2 * half) + eps)
    mine_gain = gain_ref[:, lanes(core * half, half)]
    other_gain = gain_ref[:, lanes((1 - core) * half, half)]
    mine_out[...] = (mine * scale * mine_gain).astype(jnp.bfloat16)
    other_out[...] = (other * scale * other_gain).astype(jnp.bfloat16)

    @pl.when(chip == core)
    def _():
        own_out[...] = mine_ref[:, lanes(core * quarter, quarter)]

    @pl.when(chip != core)
    def _():
        own_out[...] = other_ref[:, lanes(core * quarter, quarter)]


def norm(scalars, mine, other, gain):
    span, half = mine.shape
    return pl.pallas_call(
        norm_kernel,
        in_specs=[SMEM, VMEM, VMEM, VMEM],
        out_specs=[VMEM] * 3,
        out_shape=[
            jax.ShapeDtypeStruct((span, half), jnp.bfloat16),
            jax.ShapeDtypeStruct((span, half), jnp.bfloat16),
            jax.ShapeDtypeStruct((span, half // 2), jnp.bfloat16),
        ],
        compiler_params=pltpu.CompilerParams(vmem_limit_bytes=16 << 20),
        name="norm",
    )(scalars, mine, other, gain)


def slots(scalars_ref, table_ref, plane, share):
    core, layer = scalars_ref[1], scalars_ref[2]
    span = table_ref.shape[1]
    ids = lax.broadcasted_iota(jnp.int32, (plane, span), 0) * RING + layer
    ids = ids.astype(jnp.float32)
    member = jnp.zeros((plane, span), jnp.float32)
    weight = jnp.zeros((plane, span), jnp.float32)
    for k in range(TOP):
        hit = table_ref[k : k + 1, :] == ids
        member = jnp.where(hit, 1.0, member)
        weight = jnp.where(hit, table_ref[TOP + k : TOP + k + 1, :], weight)
    earlier = lax.broadcasted_iota(jnp.int32, (span, span), 0) < lax.broadcasted_iota(
        jnp.int32, (span, span), 1
    )
    rank = jnp.dot(
        member.astype(jnp.bfloat16),
        earlier.astype(jnp.float32).astype(jnp.bfloat16),
        preferred_element_type=jnp.float32,
    )
    slot = jnp.where(member > 0.0, rank - (core * share).astype(jnp.float32), -1.0)
    shape = (plane, share, span)
    wanted = lax.broadcasted_iota(jnp.int32, shape, 1).astype(jnp.float32)
    chosen = jnp.broadcast_to(slot[:, None, :], shape) == wanted
    return chosen, weight


def dispatch_kernel(plane, share, scalars_ref, *refs):
    count = (len(refs) - 1) // 3
    out_ref = refs[-1]
    core = scalars_ref[1]
    for r in range(count):
        table_ref, mine_ref, other_ref = refs[3 * r : 3 * r + 3]
        half = mine_ref.shape[1]
        chosen, _ = slots(scalars_ref, table_ref, plane, share)
        select = jnp.where(chosen, 1.0, 0.0).reshape(plane * share, chosen.shape[2])
        select = select.astype(jnp.bfloat16)
        for ref, which in ((mine_ref, core), (other_ref, 1 - core)):
            rows = jnp.dot(select, ref[...], preferred_element_type=jnp.float32)
            rows = rows.astype(jnp.bfloat16).reshape(plane, share, half)
            out_ref[:, r * share : (r + 1) * share, lanes(which * half, half)] = rows


def dispatch(scalars, plane, share, items):
    count = len(items)
    half = items[0][1].shape[1]
    return pl.pallas_call(
        lambda *refs: dispatch_kernel(plane, share, *refs),
        in_specs=[SMEM] + [VMEM] * (3 * count),
        out_specs=VMEM,
        out_shape=jax.ShapeDtypeStruct((plane, count * share, 2 * half), jnp.bfloat16),
        compiler_params=pltpu.CompilerParams(vmem_limit_bytes=24 << 20),
        name="dispatch",
    )(scalars, *[part for item in items for part in item])


def combine_kernel(r, plane, share, scalars_ref, table_ref, rows_ref, keep_ref, pass_ref, send_ref):
    chip, core = scalars_ref[0], scalars_ref[1]
    quarter = keep_ref.shape[1]
    chosen, weight = slots(scalars_ref, table_ref, plane, share)
    high = weight.astype(jnp.bfloat16).astype(jnp.float32)
    mixes = []
    for w in (high, weight - high):
        mix = jnp.where(chosen, jnp.broadcast_to(w[:, None, :], chosen.shape), 0.0)
        mixes.append(mix.reshape(plane * share, chosen.shape[2]).astype(jnp.bfloat16))

    def mixture(its_chip, its_core):
        rows = rows_ref[
            :, r * share : (r + 1) * share, lanes((2 * its_chip + its_core) * quarter, quarter)
        ]
        rows = rows.reshape(plane * share, quarter)
        return sum(
            lax.dot_general(mix, rows, TN, preferred_element_type=jnp.float32) for mix in mixes
        )

    keep_ref[...] = mixture(chip, core)
    pass_ref[...] = mixture(1 - chip, core)
    send_ref[:, :quarter] = mixture(chip, 1 - core).astype(jnp.bfloat16)
    send_ref[:, quarter:] = mixture(1 - chip, 1 - core).astype(jnp.bfloat16)


def combine(scalars, r, plane, share, table, rows):
    span = table.shape[1]
    quarter = rows.shape[2] // 4
    return pl.pallas_call(
        lambda *refs: combine_kernel(r, plane, share, *refs),
        in_specs=[SMEM, VMEM, VMEM],
        out_specs=[VMEM] * 3,
        out_shape=[
            jax.ShapeDtypeStruct((span, quarter), jnp.float32),
            jax.ShapeDtypeStruct((span, quarter), jnp.float32),
            jax.ShapeDtypeStruct((span, 2 * quarter), jnp.bfloat16),
        ],
        compiler_params=pltpu.CompilerParams(vmem_limit_bytes=24 << 20),
        name="combine",
    )(scalars, table, rows)


def fold_kernel(keep_ref, onward_ref, came_ref, keep_out, onward_out):
    quarter = keep_ref.shape[1]
    keep_out[...] = keep_ref[...] + came_ref[:, :quarter].astype(jnp.float32)
    onward = onward_ref[...] + came_ref[:, quarter:].astype(jnp.float32)
    onward_out[...] = onward.astype(jnp.bfloat16)


def fold(keep, onward, came):
    return pl.pallas_call(
        fold_kernel,
        in_specs=[VMEM] * 3,
        out_specs=[VMEM] * 2,
        out_shape=[
            jax.ShapeDtypeStruct(keep.shape, jnp.float32),
            jax.ShapeDtypeStruct(onward.shape, jnp.bfloat16),
        ],
        compiler_params=pltpu.CompilerParams(vmem_limit_bytes=8 << 20),
        name="fold",
    )(keep, onward, came)


def total_kernel(keep_ref, came_ref, out_ref):
    out_ref[...] = (keep_ref[...] + came_ref[...].astype(jnp.float32)).astype(jnp.bfloat16)


def total_of(keep, came):
    return pl.pallas_call(
        total_kernel,
        in_specs=[VMEM] * 2,
        out_specs=VMEM,
        out_shape=jax.ShapeDtypeStruct(keep.shape, jnp.bfloat16),
        compiler_params=pltpu.CompilerParams(vmem_limit_bytes=8 << 20),
        name="total",
    )(keep, came)


def expert_kernel(slices, x_ref, *refs):
    weights = refs[: 3 * slices]
    out_ref, held, sems = refs[3 * slices :]
    copies = [
        pltpu.make_async_copy(weights[i], held.at[i], sems.at[i]) for i in range(3 * slices)
    ]
    for copy in copies:
        copy.start()
    x = x_ref[...]
    total = None
    for j in range(slices):
        copies[3 * j].wait()
        gate = lax.dot_general(x, held[3 * j], NT, preferred_element_type=jnp.float32)
        copies[3 * j + 1].wait()
        upper = lax.dot_general(x, held[3 * j + 1], NT, preferred_element_type=jnp.float32)
        act = (gate / (1.0 + jnp.exp(-gate)) * upper).astype(jnp.bfloat16)
        copies[3 * j + 2].wait()
        part = jnp.dot(act, held[3 * j + 2], preferred_element_type=jnp.float32)
        total = part if total is None else total + part
    out_ref[...] = total.astype(jnp.bfloat16)


def expert(inbox, weights):
    rows, width = inbox.shape[0] * inbox.shape[1], inbox.shape[2]
    units = weights[0].shape[0]
    count = len(weights)
    out = pl.pallas_call(
        lambda *refs: expert_kernel(count // 3, *refs),
        in_specs=[VMEM] + [pl.BlockSpec(memory_space=pltpu.HBM)] * count,
        out_specs=VMEM,
        out_shape=jax.ShapeDtypeStruct((rows, width), jnp.bfloat16),
        scratch_shapes=[
            pltpu.VMEM((count, units, width), jnp.bfloat16),
            pltpu.SemaphoreType.DMA((count,)),
        ],
        cost_estimate=pl.CostEstimate(
            flops=2 * count * rows * width * units,
            transcendentals=rows * units * count // 3,
            bytes_accessed=2 * count * units * width + 4 * rows * width,
        ),
        name="expert",
    )(inbox.reshape(rows, width), *weights)
    return out.reshape(inbox.shape)


def stage_kernel(scalars_ref, k_ref, v_ref, ck_ref, cv_ref, *outs):
    me, length = scalars_ref[0], scalars_ref[1]
    block = k_ref.shape[0]
    last = ck_ref.shape[0] // block - 1
    for mask, out_ref in enumerate(outs):
        peer = me ^ mask
        start = pl.multiple_of(jnp.minimum(peer, last) * block, block)
        row = lax.broadcasted_iota(jnp.int32, (block, block), 0) + peer * block - length
        moved = row == lax.broadcasted_iota(jnp.int32, (block, block), 1)
        moved = jnp.where(moved, 1.0, 0.0).astype(jnp.bfloat16)
        for which, (fresh_ref, cached_ref) in enumerate(((k_ref, ck_ref), (v_ref, cv_ref))):
            fresh = jnp.dot(moved, fresh_ref[...], preferred_element_type=jnp.float32)
            kept = cached_ref[pl.ds(start, block), :].astype(jnp.float32)
            old = lax.broadcasted_iota(jnp.int32, kept.shape, 0) + peer * block < length
            out_ref[which] = jnp.where(old, kept, fresh).astype(jnp.bfloat16)


def stage(scalars, span_k, span_v, cache_k, cache_v, pieces):
    span, columns = span_k.shape
    return pl.pallas_call(
        stage_kernel,
        in_specs=[SMEM] + [VMEM] * 4,
        out_specs=[VMEM] * pieces,
        out_shape=[jax.ShapeDtypeStruct((2, span, columns), jnp.bfloat16)] * pieces,
        compiler_params=pltpu.CompilerParams(vmem_limit_bytes=32 << 20),
        name="stage",
    )(scalars, span_k, span_v, cache_k, cache_v)


def join_kernel(scalars_ref, *refs):
    out_ref = refs[-1]
    columns = refs[0].shape[2]
    for mask, ref in enumerate(refs[:-1]):
        out_ref[:, :, lanes((scalars_ref[0] ^ mask) * columns, columns)] = ref[...]


def join(scalars, pieces):
    kinds, block, columns = pieces[0].shape
    return pl.pallas_call(
        join_kernel,
        in_specs=[SMEM] + [VMEM] * len(pieces),
        out_specs=VMEM,
        out_shape=jax.ShapeDtypeStruct((kinds, block, columns * len(pieces)), jnp.bfloat16),
        compiler_params=pltpu.CompilerParams(vmem_limit_bytes=16 << 20),
        name="join",
    )(scalars, *pieces)


def flip(value, mask):
    groups = lax.axis_size("tensor")
    return lax.ppermute(value, "tensor", [(i, i ^ mask) for i in range(groups)])


def along(value, step):
    count = lax.axis_size("request")
    pairs = [(i, i // RING * RING + (i + step) % RING) for i in range(count)]
    return lax.ppermute(value, "request", pairs)


def on_device(
    hidden_in,
    span_q,
    span_k,
    span_v,
    cache_k,
    cache_v,
    cached_len,
    out_proj,
    norm_gain,
    routes,
    route_weight,
    w_gate,
    w_up,
    w_down,
):
    span, width = hidden_in.shape
    groups = lax.axis_size("tensor")
    experts = lax.axis_size("request")
    plane = experts // RING
    half = width // 2
    me = lax.axis_index("tensor")
    core = me % 2
    chip = me // 2
    layer = lax.axis_index("request") % RING
    length = cached_len[0]
    planes = [[column * RING + z for column in range(plane)] for z in range(RING)]
    scalars = jnp.stack([chip, core, layer]).astype(jnp.int32)

    def exchange(value):
        return lax.all_to_all(
            value, "request", split_axis=0, concat_axis=0, axis_index_groups=planes, tiled=True
        )

    own_w = (jnp.swapaxes(w_gate[0], 0, 1), jnp.swapaxes(w_up[0], 0, 1), w_down[0])
    near_w = tuple(flip(w, 1) for w in own_w)
    weights = own_w + near_w

    most = max(2, 2 * span * TOP // experts)
    share = most // 2
    table = jnp.concatenate([routes.T.astype(jnp.float32), route_weight.T], axis=0)
    tables = {0: table}
    for step in (1, -1, 2):
        tables[step] = along(table, step)

    keep, send = attend(
        jnp.stack([length, core]).astype(jnp.int32),
        span_q,
        span_k,
        span_v,
        cache_k[0],
        cache_v[0],
        out_proj,
    )
    keep = keep + flip(send, 1).astype(jnp.float32)
    keep = keep + flip(keep.astype(jnp.bfloat16), 2).astype(jnp.float32)
    hidden_half = lax.dynamic_slice_in_dim(hidden_in, core * half, half, 1)
    mixed_half = (hidden_half.astype(jnp.float32) + keep).astype(jnp.bfloat16)
    mine, other, own_mixed = norm(
        scalars, mixed_half, flip(mixed_half, 1), norm_gain.reshape(1, width)
    )

    tokens = {0: (mine, other)}
    for step in (1, -1, 2):
        came = along(mine, step)
        tokens[step] = (came, flip(came, 1))

    chunks = ((0,), (1, -1), (2,))
    outs = []
    for steps in chunks:
        outbox = dispatch(scalars, plane, share, [(tables[step],) + tokens[step] for step in steps])
        inbox = exchange(outbox)
        outs.append(expert(inbox, weights))

    result = own_mixed.astype(jnp.float32)
    for number in (1, 2, 0):
        returned = exchange(outs[number])
        for r, step in enumerate(chunks[number]):
            keep, onward, send = combine(scalars, r, plane, share, tables[step], returned)
            came = flip(send, 1)
            keep, onward = fold(keep, onward, came)
            came = flip(onward, 2)
            if step:
                keep = total_of(keep, came)
                keep = along(keep, -step).astype(jnp.float32)
            else:
                keep = keep + came.astype(jnp.float32)
            result = result + keep
    layer_out = result.astype(jnp.bfloat16)

    spot = jnp.stack([me, length]).astype(jnp.int32)
    pieces = stage(spot, span_k, span_v, cache_k[0], cache_v[0], groups)
    pieces = [pieces[0]] + [flip(pieces[m], m) for m in range(1, groups)]
    decode = join(spot, pieces)
    return (layer_out, decode[None])


def solution(mesh):
    in_specs = (
        P("request", None),
        P("request", "tensor"),
        P("request", "tensor"),
        P("request", "tensor"),
        P("request", None, "tensor"),
        P("request", None, "tensor"),
        P("request"),
        P("tensor", None),
        P(),
        P("request", None),
        P("request", None),
        P("request", None, "tensor"),
        P("request", None, "tensor"),
        P("request", "tensor", None),
    )
    out_specs = (P("request", "tensor"), P("request", None, "tensor", None))

    return jax.shard_map(
        on_device, mesh=mesh, in_specs=in_specs, out_specs=out_specs, check_vma=False
    )
```

```python
import jax
import jax.numpy as jnp
from jax import lax
from jax.experimental import pallas as pl
from jax.experimental.pallas import tpu as pltpu
from jax.sharding import PartitionSpec as P


HD = 128
TOP = 4
RING = 4


eps = 1e-06
neg_large = -1e30


NT = (((1,), (1,)), ((), ()))
TN = (((0,), (0,)), ((), ()))
VMEM = pl.BlockSpec(memory_space=pltpu.VMEM)
SMEM = pl.BlockSpec(memory_space=pltpu.SMEM)


def lanes(start, size):
    return pl.ds(pl.multiple_of(start, 128), size)


def attend_kernel(
    scalars_ref, q_ref, k_ref, v_ref, ck_ref, cv_ref, w_ref, keep_ref, send_ref, part_ref
):
    head = pl.program_id(0)
    length, core = scalars_ref[0], scalars_ref[1]
    query = q_ref[...]
    scale = HD ** (-0.5)
    old = lax.dot_general(query, ck_ref[...], NT, preferred_element_type=jnp.float32) * scale
    new = lax.dot_general(query, k_ref[...], NT, preferred_element_type=jnp.float32) * scale
    old = jnp.where(lax.broadcasted_iota(jnp.int32, old.shape, 1) < length, old, neg_large)
    rows = lax.broadcasted_iota(jnp.int32, new.shape, 0)
    new = jnp.where(lax.broadcasted_iota(jnp.int32, new.shape, 1) <= rows, new, neg_large)
    top = jnp.maximum(
        jnp.max(old, axis=1, keepdims=True), jnp.max(new, axis=1, keepdims=True)
    )
    old = jnp.exp(old - top)
    new = jnp.exp(new - top)
    inverse = 1.0 / (jnp.sum(old, axis=1, keepdims=True) + jnp.sum(new, axis=1, keepdims=True))
    attended = jnp.dot(
        (old * inverse).astype(jnp.bfloat16), cv_ref[...], preferred_element_type=jnp.float32
    ) + jnp.dot(
        (new * inverse).astype(jnp.bfloat16), v_ref[...], preferred_element_type=jnp.float32
    )
    part = jnp.dot(
        attended.astype(jnp.bfloat16), w_ref[...], preferred_element_type=jnp.float32
    )

    @pl.when(head == 0)
    def _():
        part_ref[...] = part

    @pl.when(head > 0)
    def _():
        part_ref[...] += part

    @pl.when(head == pl.num_programs(0) - 1)
    def _():
        half = keep_ref.shape[1]
        keep_ref[...] = part_ref[:, lanes(core * half, half)]
        send_ref[...] = part_ref[:, lanes((1 - core) * half, half)].astype(jnp.bfloat16)


def attend(scalars, span_q, span_k, span_v, cache_k, cache_v, out_proj):
    span, columns = span_q.shape
    prior = cache_k.shape[0]
    width = out_proj.shape[1]
    heads = columns // HD
    fresh = pl.BlockSpec((span, HD), lambda h, n: (0, h))
    cached = pl.BlockSpec((prior, HD), lambda h, n: (0, h))
    halves = pl.BlockSpec((span, width // 2), lambda h, n: (0, 0))
    return pl.pallas_call(
        attend_kernel,
        grid_spec=pltpu.PrefetchScalarGridSpec(
            num_scalar_prefetch=1,
            grid=(heads,),
            in_specs=[
                fresh,
                fresh,
                fresh,
                cached,
                cached,
                pl.BlockSpec((HD, width), lambda h, n: (h, 0)),
            ],
            out_specs=[halves, halves],
            scratch_shapes=[pltpu.VMEM((span, width), jnp.float32)],
        ),
        out_shape=[
            jax.ShapeDtypeStruct((span, width // 2), jnp.float32),
            jax.ShapeDtypeStruct((span, width // 2), jnp.bfloat16),
        ],
        cost_estimate=pl.CostEstimate(
            flops=heads * span * (4 * (prior + span) * HD + 2 * HD * width),
            transcendentals=heads * span * (prior + span),
            bytes_accessed=9 << 20,
        ),
        name="attend",
    )(scalars, span_q, span_k, span_v, cache_k, cache_v, out_proj)


def norm_kernel(scalars_ref, mine_ref, other_ref, gain_ref, mine_out, other_out, own_out):
    chip, core = scalars_ref[0], scalars_ref[1]
    half = mine_ref.shape[1]
    quarter = half // 2
    mine = mine_ref[...].astype(jnp.float32)
    other = other_ref[...].astype(jnp.float32)
    total = jnp.sum(mine * mine, axis=1, keepdims=True) + jnp.sum(
        other * other, axis=1, keepdims=True
    )
    scale = lax.rsqrt(total / (2 * half) + eps)
    mine_gain = gain_ref[:, lanes(core * half, half)]
    other_gain = gain_ref[:, lanes((1 - core) * half, half)]
    mine_out[...] = (mine * scale * mine_gain).astype(jnp.bfloat16)
    other_out[...] = (other * scale * other_gain).astype(jnp.bfloat16)

    @pl.when(chip == core)
    def _():
        own_out[...] = mine_ref[:, lanes(core * quarter, quarter)]

    @pl.when(chip != core)
    def _():
        own_out[...] = other_ref[:, lanes(core * quarter, quarter)]


def norm(scalars, mine, other, gain):
    span, half = mine.shape
    return pl.pallas_call(
        norm_kernel,
        in_specs=[SMEM, VMEM, VMEM, VMEM],
        out_specs=[VMEM] * 3,
        out_shape=[
            jax.ShapeDtypeStruct((span, half), jnp.bfloat16),
            jax.ShapeDtypeStruct((span, half), jnp.bfloat16),
            jax.ShapeDtypeStruct((span, half // 2), jnp.bfloat16),
        ],
        compiler_params=pltpu.CompilerParams(vmem_limit_bytes=16 << 20),
        name="norm",
    )(scalars, mine, other, gain)


def slots(scalars_ref, table_ref, plane, share):
    core, layer = scalars_ref[1], scalars_ref[2]
    span = table_ref.shape[1]
    ids = lax.broadcasted_iota(jnp.int32, (plane, span), 0) * RING + layer
    ids = ids.astype(jnp.float32)
    member = jnp.zeros((plane, span), jnp.float32)
    weight = jnp.zeros((plane, span), jnp.float32)
    for k in range(TOP):
        hit = table_ref[k : k + 1, :] == ids
        member = jnp.where(hit, 1.0, member)
        weight = jnp.where(hit, table_ref[TOP + k : TOP + k + 1, :], weight)
    earlier = lax.broadcasted_iota(jnp.int32, (span, span), 0) < lax.broadcasted_iota(
        jnp.int32, (span, span), 1
    )
    rank = jnp.dot(
        member.astype(jnp.bfloat16),
        earlier.astype(jnp.float32).astype(jnp.bfloat16),
        preferred_element_type=jnp.float32,
    )
    slot = jnp.where(member > 0.0, rank - (core * share).astype(jnp.float32), -1.0)
    shape = (plane, share, span)
    wanted = lax.broadcasted_iota(jnp.int32, shape, 1).astype(jnp.float32)
    chosen = jnp.broadcast_to(slot[:, None, :], shape) == wanted
    return chosen, weight


def dispatch_kernel(plane, share, scalars_ref, *refs):
    count = (len(refs) - 1) // 3
    out_ref = refs[-1]
    core = scalars_ref[1]
    for r in range(count):
        table_ref, mine_ref, other_ref = refs[3 * r : 3 * r + 3]
        half = mine_ref.shape[1]
        chosen, _ = slots(scalars_ref, table_ref, plane, share)
        select = jnp.where(chosen, 1.0, 0.0).reshape(plane * share, chosen.shape[2])
        select = select.astype(jnp.bfloat16)
        for ref, which in ((mine_ref, core), (other_ref, 1 - core)):
            rows = jnp.dot(select, ref[...], preferred_element_type=jnp.float32)
            rows = rows.astype(jnp.bfloat16).reshape(plane, share, half)
            out_ref[:, r * share : (r + 1) * share, lanes(which * half, half)] = rows


def dispatch(scalars, plane, share, items):
    count = len(items)
    half = items[0][1].shape[1]
    return pl.pallas_call(
        lambda *refs: dispatch_kernel(plane, share, *refs),
        in_specs=[SMEM] + [VMEM] * (3 * count),
        out_specs=VMEM,
        out_shape=jax.ShapeDtypeStruct((plane, count * share, 2 * half), jnp.bfloat16),
        compiler_params=pltpu.CompilerParams(vmem_limit_bytes=24 << 20),
        name="dispatch",
    )(scalars, *[part for item in items for part in item])


def combine_kernel(kind, count, plane, share, scalars_ref, *refs):
    tables, rows_ref = refs[:count], refs[count]
    keep_ref, pass_ref, send_ref = refs[count + 1 :]
    chip, core = scalars_ref[0], scalars_ref[1]
    quarter = rows_ref.shape[2] // 4

    def mixer(table, r):
        chosen, weight = slots(scalars_ref, table, plane, share)
        high = weight.astype(jnp.bfloat16).astype(jnp.float32)
        mixes = []
        for w in (high, weight - high):
            mix = jnp.where(chosen, jnp.broadcast_to(w[:, None, :], chosen.shape), 0.0)
            mixes.append(mix.reshape(plane * share, chosen.shape[2]).astype(jnp.bfloat16))

        def mixture(its_chip, its_core):
            start = pl.multiple_of(r * share, share)
            columns = lanes((2 * its_chip + its_core) * quarter, quarter)
            rows = rows_ref[:, pl.ds(start, share), columns].reshape(plane * share, quarter)
            return sum(
                lax.dot_general(mix, rows, TN, preferred_element_type=jnp.float32) for mix in mixes
            )

        return mixture

    if kind == "pair":
        down, up = tables[0][...], tables[1][...]
        here = jnp.where(chip == 1, 1, 0)
        keeper = mixer(jnp.where(chip == 1, up, down), here)
        passer = mixer(jnp.where(chip == 1, down, up), 1 - here)
        parts = [(keeper, 0), (keeper, 1), (passer, 0), (passer, 1)]
    else:
        only = mixer(tables[0][...], 0)
        parts = [(only, chip), (only, 1 - chip)] if kind == "own" else [(only, 1 - chip), (only, chip)]
    each = len(parts) // 2
    for i, (mixture, its_chip) in enumerate(parts):
        out_ref = keep_ref if i < each else pass_ref
        place = i % each * quarter
        out_ref[:, place : place + quarter] = mixture(its_chip, core)
        sent = mixture(its_chip, 1 - core)
        send_ref[:, i * quarter : (i + 1) * quarter] = sent.astype(jnp.bfloat16)


def combine(kind, scalars, plane, share, tables, rows):
    span = tables[0].shape[1]
    width = rows.shape[2] // 4 * (2 if kind == "pair" else 1)
    count = len(tables)
    return pl.pallas_call(
        lambda *refs: combine_kernel(kind, count, plane, share, *refs),
        in_specs=[SMEM] + [VMEM] * (count + 1),
        out_specs=[VMEM] * 3,
        out_shape=[
            jax.ShapeDtypeStruct((span, width), jnp.float32),
            jax.ShapeDtypeStruct((span, width), jnp.float32),
            jax.ShapeDtypeStruct((span, 2 * width), jnp.bfloat16),
        ],
        compiler_params=pltpu.CompilerParams(vmem_limit_bytes=24 << 20),
        name="combine",
    )(scalars, *tables, rows)


def close_kernel(scalars_ref, keep_ref, onward_ref, came_ref, home_ref, keep_out, onward_out):
    chip = scalars_ref[0]
    quarter = keep_ref.shape[1]
    mine = home_ref[:, lanes(chip * quarter, quarter)].astype(jnp.float32)
    other = home_ref[:, lanes((1 - chip) * quarter, quarter)].astype(jnp.float32)
    keep_out[...] = keep_ref[...] + came_ref[:, :quarter].astype(jnp.float32) + mine
    onward = onward_ref[...] + came_ref[:, quarter:].astype(jnp.float32) + other
    onward_out[...] = onward.astype(jnp.bfloat16)


def close(scalars, keep, onward, came, home):
    return pl.pallas_call(
        close_kernel,
        in_specs=[SMEM] + [VMEM] * 4,
        out_specs=[VMEM] * 2,
        out_shape=[
            jax.ShapeDtypeStruct(keep.shape, jnp.float32),
            jax.ShapeDtypeStruct(onward.shape, jnp.bfloat16),
        ],
        compiler_params=pltpu.CompilerParams(vmem_limit_bytes=8 << 20),
        name="close",
    )(scalars, keep, onward, came, home)


def fold_kernel(keep_ref, onward_ref, came_ref, keep_out, onward_out):
    quarter = keep_ref.shape[1]
    keep_out[...] = keep_ref[...] + came_ref[:, :quarter].astype(jnp.float32)
    onward = onward_ref[...] + came_ref[:, quarter:].astype(jnp.float32)
    onward_out[...] = onward.astype(jnp.bfloat16)


def fold(keep, onward, came):
    return pl.pallas_call(
        fold_kernel,
        in_specs=[VMEM] * 3,
        out_specs=[VMEM] * 2,
        out_shape=[
            jax.ShapeDtypeStruct(keep.shape, jnp.float32),
            jax.ShapeDtypeStruct(onward.shape, jnp.bfloat16),
        ],
        compiler_params=pltpu.CompilerParams(vmem_limit_bytes=8 << 20),
        name="fold",
    )(keep, onward, came)


def total_kernel(keep_ref, came_ref, out_ref):
    out_ref[...] = (keep_ref[...] + came_ref[...].astype(jnp.float32)).astype(jnp.bfloat16)


def total_of(keep, came):
    return pl.pallas_call(
        total_kernel,
        in_specs=[VMEM] * 2,
        out_specs=VMEM,
        out_shape=jax.ShapeDtypeStruct(keep.shape, jnp.bfloat16),
        compiler_params=pltpu.CompilerParams(vmem_limit_bytes=8 << 20),
        name="total",
    )(keep, came)


def expert_kernel(slices, x_ref, *refs):
    weights = refs[: 3 * slices]
    out_ref, held, total, sems = refs[3 * slices :]
    block = total.shape[0]
    copies = [
        pltpu.make_async_copy(weights[i], held.at[i], sems.at[i]) for i in range(3 * slices)
    ]
    for copy in copies:
        copy.start()

    def step(i, carry):
        number, j = i // slices, i % slices
        start = pl.multiple_of(number * block, block)

        def arrive(k):
            @pl.when(number == 0)
            def _():
                pltpu.make_async_copy(weights[k], held.at[3 * j + k], sems.at[3 * j + k]).wait()

        x = x_ref[pl.ds(start, block), :]
        arrive(0)
        gate = lax.dot_general(x, held[3 * j], NT, preferred_element_type=jnp.float32)
        arrive(1)
        upper = lax.dot_general(x, held[3 * j + 1], NT, preferred_element_type=jnp.float32)
        act = (gate / (1.0 + jnp.exp(-gate)) * upper).astype(jnp.bfloat16)
        arrive(2)
        part = jnp.dot(act, held[3 * j + 2], preferred_element_type=jnp.float32)

        @pl.when(j == 0)
        def _():
            total[...] = part

        @pl.when((j > 0) & (j < slices - 1))
        def _():
            total[...] += part

        @pl.when(j == slices - 1)
        def _():
            out_ref[pl.ds(start, block), :] = (total[...] + part).astype(jnp.bfloat16)

        return carry

    lax.fori_loop(0, x_ref.shape[0] // block * slices, step, 0)


def expert(inbox, weights):
    rows, width = inbox.shape[0] * inbox.shape[1], inbox.shape[2]
    units = weights[0].shape[0]
    count = len(weights)
    block = min(rows, 256)
    out = pl.pallas_call(
        lambda *refs: expert_kernel(count // 3, *refs),
        in_specs=[VMEM] + [pl.BlockSpec(memory_space=pl.ANY)] * count,
        out_specs=VMEM,
        out_shape=jax.ShapeDtypeStruct((rows, width), jnp.bfloat16),
        scratch_shapes=[
            pltpu.VMEM((count, units, width), jnp.bfloat16),
            pltpu.VMEM((block, width), jnp.float32),
            pltpu.SemaphoreType.DMA((count,)),
        ],
        cost_estimate=pl.CostEstimate(
            flops=2 * count * rows * width * units,
            transcendentals=rows * units * count // 3,
            bytes_accessed=2 * count * units * width + 4 * rows * width,
        ),
        name="expert",
    )(inbox.reshape(rows, width), *weights)
    return out.reshape(inbox.shape)


def stage_kernel(scalars_ref, k_ref, v_ref, ck_ref, cv_ref, *outs):
    me, length = scalars_ref[0], scalars_ref[1]
    block = k_ref.shape[0]
    last = ck_ref.shape[0] // block - 1
    for mask, out_ref in enumerate(outs):
        peer = me ^ mask
        start = pl.multiple_of(jnp.minimum(peer, last) * block, block)
        row = lax.broadcasted_iota(jnp.int32, (block, block), 0) + peer * block - length
        moved = row == lax.broadcasted_iota(jnp.int32, (block, block), 1)
        moved = jnp.where(moved, 1.0, 0.0).astype(jnp.bfloat16)
        for which, (fresh_ref, cached_ref) in enumerate(((k_ref, ck_ref), (v_ref, cv_ref))):
            fresh = jnp.dot(moved, fresh_ref[...], preferred_element_type=jnp.float32)
            kept = cached_ref[pl.ds(start, block), :].astype(jnp.float32)
            old = lax.broadcasted_iota(jnp.int32, kept.shape, 0) + peer * block < length
            out_ref[which] = jnp.where(old, kept, fresh).astype(jnp.bfloat16)


def stage(scalars, span_k, span_v, cache_k, cache_v, pieces):
    span, columns = span_k.shape
    return pl.pallas_call(
        stage_kernel,
        in_specs=[SMEM] + [VMEM] * 4,
        out_specs=[VMEM] * pieces,
        out_shape=[jax.ShapeDtypeStruct((2, span, columns), jnp.bfloat16)] * pieces,
        compiler_params=pltpu.CompilerParams(vmem_limit_bytes=32 << 20),
        name="stage",
    )(scalars, span_k, span_v, cache_k, cache_v)


def join_kernel(scalars_ref, *refs):
    out_ref = refs[-1]
    columns = refs[0].shape[2]
    for mask, ref in enumerate(refs[:-1]):
        out_ref[:, :, lanes((scalars_ref[0] ^ mask) * columns, columns)] = ref[...]


def join(scalars, pieces):
    kinds, block, columns = pieces[0].shape
    return pl.pallas_call(
        join_kernel,
        in_specs=[SMEM] + [VMEM] * len(pieces),
        out_specs=VMEM,
        out_shape=jax.ShapeDtypeStruct((kinds, block, columns * len(pieces)), jnp.bfloat16),
        compiler_params=pltpu.CompilerParams(vmem_limit_bytes=16 << 20),
        name="join",
    )(scalars, *pieces)


def flip(value, mask):
    groups = lax.axis_size("tensor")
    return lax.ppermute(value, "tensor", [(i, i ^ mask) for i in range(groups)])


def along(value, step):
    count = lax.axis_size("request")
    pairs = [(i, i // RING * RING + (i + step) % RING) for i in range(count)]
    return lax.ppermute(value, "request", pairs)


def homeward(value, gap):
    count, groups = lax.axis_size("request"), lax.axis_size("tensor")
    pairs = []
    for i in range(count):
        for t in range(groups):
            to = (i + (gap if t // 2 else -gap)) % RING + i // RING * RING
            pairs.append((t * count + i, (t ^ 2) * count + to))
    return lax.ppermute(value, ("tensor", "request"), pairs)


def on_device(
    hidden_in,
    span_q,
    span_k,
    span_v,
    cache_k,
    cache_v,
    cached_len,
    out_proj,
    norm_gain,
    routes,
    route_weight,
    w_gate,
    w_up,
    w_down,
):
    span, width = hidden_in.shape
    groups = lax.axis_size("tensor")
    experts = lax.axis_size("request")
    plane = experts // RING
    half = width // 2
    me = lax.axis_index("tensor")
    core = me % 2
    chip = me // 2
    layer = lax.axis_index("request") % RING
    length = cached_len[0]
    planes = [[column * RING + z for column in range(plane)] for z in range(RING)]
    scalars = jnp.stack([chip, core, layer]).astype(jnp.int32)

    def exchange(value):
        return lax.all_to_all(
            value, "request", split_axis=0, concat_axis=0, axis_index_groups=planes, tiled=True
        )

    own_w = (jnp.swapaxes(w_gate[0], 0, 1), jnp.swapaxes(w_up[0], 0, 1), w_down[0])
    near_w = tuple(flip(w, 1) for w in own_w)
    weights = own_w + near_w

    most = max(2, 2 * span * TOP // experts)
    share = most // 2
    table = jnp.concatenate([routes.T.astype(jnp.float32), route_weight.T], axis=0)
    tables = {0: table}
    for step in (1, -1, 2):
        tables[step] = along(table, step)

    keep, send = attend(
        jnp.stack([length, core]).astype(jnp.int32),
        span_q,
        span_k,
        span_v,
        cache_k[0],
        cache_v[0],
        out_proj,
    )
    keep = keep + flip(send, 1).astype(jnp.float32)
    keep = keep + flip(keep.astype(jnp.bfloat16), 2).astype(jnp.float32)
    hidden_half = lax.dynamic_slice_in_dim(hidden_in, core * half, half, 1)
    mixed_half = (hidden_half.astype(jnp.float32) + keep).astype(jnp.bfloat16)
    mine, other, own_mixed = norm(
        scalars, mixed_half, flip(mixed_half, 1), norm_gain.reshape(1, width)
    )

    tokens = {0: (mine, other)}
    for step in (1, -1, 2):
        came = along(mine, step)
        tokens[step] = (came, flip(came, 1))

    chunks = ((0,), (1, -1), (2,))
    outs = []
    for steps in chunks:
        outbox = dispatch(scalars, plane, share, [(tables[step],) + tokens[step] for step in steps])
        inbox = exchange(outbox)
        outs.append(expert(inbox, weights))

    def gather(kind, number, steps):
        returned = exchange(outs[number])
        keep, onward, send = combine(
            kind, scalars, plane, share, [tables[step] for step in steps], returned
        )
        return keep, onward, flip(send, 1)

    homes = []
    for kind, number, gap in (("pair", 1, 1), ("far", 2, 2)):
        keep, onward, came = gather(kind, number, chunks[number])
        keep, onward = fold(keep, onward, came)
        came = flip(onward, 2)
        keep = total_of(keep, came)
        homes.append(homeward(keep, gap))
    keep, onward, came = gather("own", 0, chunks[0])
    keep, onward = close(scalars, keep, onward, came, homes[0])
    came = flip(onward, 2)
    result = own_mixed.astype(jnp.float32) + keep
    result = result + came.astype(jnp.float32) + homes[1].astype(jnp.float32)
    layer_out = result.astype(jnp.bfloat16)

    spot = jnp.stack([me, length]).astype(jnp.int32)
    pieces = stage(spot, span_k, span_v, cache_k[0], cache_v[0], groups)
    pieces = [pieces[0]] + [flip(pieces[m], m) for m in range(1, groups)]
    decode = join(spot, pieces)
    return (layer_out, decode[None])


def solution(mesh):
    in_specs = (
        P("request", None),
        P("request", "tensor"),
        P("request", "tensor"),
        P("request", "tensor"),
        P("request", None, "tensor"),
        P("request", None, "tensor"),
        P("request"),
        P("tensor", None),
        P(),
        P("request", None),
        P("request", None),
        P("request", None, "tensor"),
        P("request", None, "tensor"),
        P("request", "tensor", None),
    )
    out_specs = (P("request", "tensor"), P("request", None, "tensor", None))

    return jax.shard_map(
        on_device, mesh=mesh, in_specs=in_specs, out_specs=out_specs, check_vma=False
    )
```

```python
import jax
import jax.numpy as jnp
from jax import lax
from jax.experimental import pallas as pl
from jax.experimental.pallas import tpu as pltpu
from jax.sharding import PartitionSpec as P


HD = 128
TOP = 4
RING = 4


eps = 1e-06
neg_large = -1e30


NT = (((1,), (1,)), ((), ()))
TN = (((0,), (0,)), ((), ()))
VMEM = pl.BlockSpec(memory_space=pltpu.VMEM)
SMEM = pl.BlockSpec(memory_space=pltpu.SMEM)


def lanes(start, size):
    return pl.ds(pl.multiple_of(start, 128), size)


def attend_kernel(scalars_ref, q_ref, k_ref, v_ref, ck_ref, cv_ref, w_ref, *refs):
    outs, part_ref = refs[:-1], refs[-1]
    group = pl.program_id(0)
    length, core = scalars_ref[0], scalars_ref[1]
    scale = HD ** (-0.5)
    attended = []
    for head in range(q_ref.shape[1] // HD):
        own = slice(head * HD, (head + 1) * HD)
        query = q_ref[:, own]
        old = lax.dot_general(query, ck_ref[:, own], NT, preferred_element_type=jnp.float32) * scale
        new = lax.dot_general(query, k_ref[:, own], NT, preferred_element_type=jnp.float32) * scale
        old = jnp.where(lax.broadcasted_iota(jnp.int32, old.shape, 1) < length, old, neg_large)
        rows = lax.broadcasted_iota(jnp.int32, new.shape, 0)
        new = jnp.where(lax.broadcasted_iota(jnp.int32, new.shape, 1) <= rows, new, neg_large)
        top = jnp.maximum(
            jnp.max(old, axis=1, keepdims=True), jnp.max(new, axis=1, keepdims=True)
        )
        old = jnp.exp(old - top)
        new = jnp.exp(new - top)
        total = jnp.sum(old, axis=1, keepdims=True) + jnp.sum(new, axis=1, keepdims=True)
        inverse = 1.0 / total
        result = jnp.dot(
            (old * inverse).astype(jnp.bfloat16), cv_ref[:, own], preferred_element_type=jnp.float32
        ) + jnp.dot(
            (new * inverse).astype(jnp.bfloat16), v_ref[:, own], preferred_element_type=jnp.float32
        )
        attended.append(result.astype(jnp.bfloat16))
    part = jnp.dot(
        jnp.concatenate(attended, axis=1), w_ref[...], preferred_element_type=jnp.float32
    )

    @pl.when(group == 0)
    def _():
        part_ref[...] = part

    @pl.when(group > 0)
    def _():
        part_ref[...] += part

    @pl.when(group == pl.num_programs(0) - 1)
    def _():
        rows, half = outs[0].shape
        for i in range(len(outs) // 2):
            keep_ref, send_ref = outs[2 * i : 2 * i + 2]
            own = slice(i * rows, (i + 1) * rows)
            keep_ref[...] = part_ref[own, lanes(core * half, half)]
            send_ref[...] = part_ref[own, lanes((1 - core) * half, half)].astype(jnp.bfloat16)


def attend(scalars, span_q, span_k, span_v, cache_k, cache_v, out_proj, pieces):
    span, columns = span_q.shape
    prior = cache_k.shape[0]
    width = out_proj.shape[1]
    heads = columns // HD
    wide = 2 * HD if heads % 2 == 0 else HD
    rows = span // pieces
    fresh = pl.BlockSpec((span, wide), lambda h, n: (0, h))
    cached = pl.BlockSpec((prior, wide), lambda h, n: (0, h))
    halves = pl.BlockSpec((rows, width // 2), lambda h, n: (0, 0))
    out = [
        jax.ShapeDtypeStruct((rows, width // 2), jnp.float32),
        jax.ShapeDtypeStruct((rows, width // 2), jnp.bfloat16),
    ]
    return pl.pallas_call(
        attend_kernel,
        grid_spec=pltpu.PrefetchScalarGridSpec(
            num_scalar_prefetch=1,
            grid=(columns // wide,),
            in_specs=[
                fresh,
                fresh,
                fresh,
                cached,
                cached,
                pl.BlockSpec((wide, width), lambda h, n: (h, 0)),
            ],
            out_specs=[halves] * (2 * pieces),
            scratch_shapes=[pltpu.VMEM((span, width), jnp.float32)],
        ),
        out_shape=out * pieces,
        cost_estimate=pl.CostEstimate(
            flops=heads * span * (4 * (prior + span) * HD + 2 * HD * width),
            transcendentals=heads * span * (prior + span),
            bytes_accessed=9 << 20,
        ),
        name="attend",
    )(scalars, span_q, span_k, span_v, cache_k, cache_v, out_proj)


def mixed_kernel(scalars_ref, hidden_ref, part_ref, came_ref, out_ref):
    total = hidden_ref[...].astype(jnp.float32) + part_ref[...]
    out_ref[...] = (total + came_ref[...].astype(jnp.float32)).astype(jnp.bfloat16)


def mixed_of(scalars, piece, hidden, part, came):
    rows, half = part.shape
    whole = pl.BlockSpec((rows, half), lambda i, n: (0, 0))
    return pl.pallas_call(
        mixed_kernel,
        grid_spec=pltpu.PrefetchScalarGridSpec(
            num_scalar_prefetch=1,
            grid=(1,),
            in_specs=[pl.BlockSpec((rows, half), lambda i, n: (piece, n[1])), whole, whole],
            out_specs=whole,
        ),
        out_shape=jax.ShapeDtypeStruct((rows, half), jnp.bfloat16),
        compiler_params=pltpu.CompilerParams(vmem_limit_bytes=8 << 20),
        name="mixed",
    )(scalars, hidden, part, came)


def norm_kernel(scalars_ref, mine_ref, other_ref, gain_ref, mine_out, other_out, own_out):
    chip, core = scalars_ref[0], scalars_ref[1]
    half = mine_ref.shape[1]
    quarter = half // 2
    mine = mine_ref[...].astype(jnp.float32)
    other = other_ref[...].astype(jnp.float32)
    total = jnp.sum(mine * mine, axis=1, keepdims=True) + jnp.sum(
        other * other, axis=1, keepdims=True
    )
    scale = lax.rsqrt(total / (2 * half) + eps)
    mine_gain = gain_ref[:, lanes(core * half, half)]
    other_gain = gain_ref[:, lanes((1 - core) * half, half)]
    mine_out[...] = (mine * scale * mine_gain).astype(jnp.bfloat16)
    other_out[...] = (other * scale * other_gain).astype(jnp.bfloat16)

    @pl.when(chip == core)
    def _():
        own_out[...] = mine_ref[:, lanes(core * quarter, quarter)]

    @pl.when(chip != core)
    def _():
        own_out[...] = other_ref[:, lanes(core * quarter, quarter)]


def norm(scalars, mine, other, gain):
    span, half = mine.shape
    return pl.pallas_call(
        norm_kernel,
        in_specs=[SMEM, VMEM, VMEM, VMEM],
        out_specs=[VMEM] * 3,
        out_shape=[
            jax.ShapeDtypeStruct((span, half), jnp.bfloat16),
            jax.ShapeDtypeStruct((span, half), jnp.bfloat16),
            jax.ShapeDtypeStruct((span, half // 2), jnp.bfloat16),
        ],
        compiler_params=pltpu.CompilerParams(vmem_limit_bytes=16 << 20),
        name="norm",
    )(scalars, mine, other, gain)


def slots(scalars_ref, table_ref, plane, share):
    core, layer = scalars_ref[1], scalars_ref[2]
    span = table_ref.shape[1]
    ids = lax.broadcasted_iota(jnp.int32, (plane, span), 0) * RING + layer
    ids = ids.astype(jnp.float32)
    member = jnp.zeros((plane, span), jnp.float32)
    weight = jnp.zeros((plane, span), jnp.float32)
    for k in range(TOP):
        hit = table_ref[k : k + 1, :] == ids
        member = jnp.where(hit, 1.0, member)
        weight = jnp.where(hit, table_ref[TOP + k : TOP + k + 1, :], weight)
    earlier = lax.broadcasted_iota(jnp.int32, (span, span), 0) < lax.broadcasted_iota(
        jnp.int32, (span, span), 1
    )
    rank = jnp.dot(
        member.astype(jnp.bfloat16),
        earlier.astype(jnp.float32).astype(jnp.bfloat16),
        preferred_element_type=jnp.float32,
    )
    slot = jnp.where(member > 0.0, rank - (core * share).astype(jnp.float32), -1.0)
    shape = (plane, share, span)
    wanted = lax.broadcasted_iota(jnp.int32, shape, 1).astype(jnp.float32)
    chosen = jnp.broadcast_to(slot[:, None, :], shape) == wanted
    return chosen, weight


def dispatch_kernel(plane, share, scalars_ref, *refs):
    count = (len(refs) - 1) // 3
    out_ref = refs[-1]
    core = scalars_ref[1]
    for r in range(count):
        table_ref, mine_ref, other_ref = refs[3 * r : 3 * r + 3]
        half = mine_ref.shape[1]
        chosen, _ = slots(scalars_ref, table_ref, plane, share)
        select = jnp.where(chosen, 1.0, 0.0).reshape(plane * share, chosen.shape[2])
        select = select.astype(jnp.bfloat16)
        for ref, which in ((mine_ref, core), (other_ref, 1 - core)):
            rows = jnp.dot(select, ref[...], preferred_element_type=jnp.float32)
            rows = rows.astype(jnp.bfloat16).reshape(plane, share, half)
            out_ref[:, r * share : (r + 1) * share, lanes(which * half, half)] = rows


def dispatch(scalars, plane, share, items):
    count = len(items)
    half = items[0][1].shape[1]
    return pl.pallas_call(
        lambda *refs: dispatch_kernel(plane, share, *refs),
        in_specs=[SMEM] + [VMEM] * (3 * count),
        out_specs=VMEM,
        out_shape=jax.ShapeDtypeStruct((plane, count * share, 2 * half), jnp.bfloat16),
        compiler_params=pltpu.CompilerParams(vmem_limit_bytes=24 << 20),
        name="dispatch",
    )(scalars, *[part for item in items for part in item])


def combine_kernel(kind, count, plane, share, scalars_ref, *refs):
    tables, rows_ref = refs[:count], refs[count]
    keep_ref, pass_ref, send_ref = refs[count + 1 :]
    chip, core = scalars_ref[0], scalars_ref[1]
    quarter = rows_ref.shape[2] // 4

    def mixer(table, r):
        chosen, weight = slots(scalars_ref, table, plane, share)
        high = weight.astype(jnp.bfloat16).astype(jnp.float32)
        mixes = []
        for w in (high, weight - high):
            mix = jnp.where(chosen, jnp.broadcast_to(w[:, None, :], chosen.shape), 0.0)
            mixes.append(mix.reshape(plane * share, chosen.shape[2]).astype(jnp.bfloat16))

        def mixture(its_chip, its_core):
            start = pl.multiple_of(r * share, share)
            columns = lanes((2 * its_chip + its_core) * quarter, quarter)
            rows = rows_ref[:, pl.ds(start, share), columns].reshape(plane * share, quarter)
            return sum(
                lax.dot_general(mix, rows, TN, preferred_element_type=jnp.float32) for mix in mixes
            )

        return mixture

    if kind == "pair":
        down, up = tables[0][...], tables[1][...]
        here = jnp.where(chip == 1, 1, 0)
        keeper = mixer(jnp.where(chip == 1, up, down), here)
        passer = mixer(jnp.where(chip == 1, down, up), 1 - here)
        parts = [(keeper, 0), (keeper, 1), (passer, 0), (passer, 1)]
    else:
        only = mixer(tables[0][...], 0)
        parts = [(only, chip), (only, 1 - chip)] if kind == "own" else [(only, 1 - chip), (only, chip)]
    each = len(parts) // 2
    for i, (mixture, its_chip) in enumerate(parts):
        out_ref = keep_ref if i < each else pass_ref
        place = i % each * quarter
        out_ref[:, place : place + quarter] = mixture(its_chip, core)
        sent = mixture(its_chip, 1 - core)
        send_ref[:, i * quarter : (i + 1) * quarter] = sent.astype(jnp.bfloat16)


def combine(kind, scalars, plane, share, tables, rows):
    span = tables[0].shape[1]
    width = rows.shape[2] // 4 * (2 if kind == "pair" else 1)
    count = len(tables)
    return pl.pallas_call(
        lambda *refs: combine_kernel(kind, count, plane, share, *refs),
        in_specs=[SMEM] + [VMEM] * (count + 1),
        out_specs=[VMEM] * 3,
        out_shape=[
            jax.ShapeDtypeStruct((span, width), jnp.float32),
            jax.ShapeDtypeStruct((span, width), jnp.float32),
            jax.ShapeDtypeStruct((span, 2 * width), jnp.bfloat16),
        ],
        compiler_params=pltpu.CompilerParams(vmem_limit_bytes=24 << 20),
        name="combine",
    )(scalars, *tables, rows)


def close_kernel(scalars_ref, keep_ref, onward_ref, came_ref, home_ref, keep_out, onward_out):
    chip = scalars_ref[0]
    quarter = keep_ref.shape[1]
    mine = home_ref[:, lanes(chip * quarter, quarter)].astype(jnp.float32)
    other = home_ref[:, lanes((1 - chip) * quarter, quarter)].astype(jnp.float32)
    keep_out[...] = keep_ref[...] + came_ref[:, :quarter].astype(jnp.float32) + mine
    onward = onward_ref[...] + came_ref[:, quarter:].astype(jnp.float32) + other
    onward_out[...] = onward.astype(jnp.bfloat16)


def close(scalars, keep, onward, came, home):
    return pl.pallas_call(
        close_kernel,
        in_specs=[SMEM] + [VMEM] * 4,
        out_specs=[VMEM] * 2,
        out_shape=[
            jax.ShapeDtypeStruct(keep.shape, jnp.float32),
            jax.ShapeDtypeStruct(onward.shape, jnp.bfloat16),
        ],
        compiler_params=pltpu.CompilerParams(vmem_limit_bytes=8 << 20),
        name="close",
    )(scalars, keep, onward, came, home)


def fold_kernel(keep_ref, onward_ref, came_ref, keep_out, onward_out):
    quarter = keep_ref.shape[1]
    keep_out[...] = keep_ref[...] + came_ref[:, :quarter].astype(jnp.float32)
    onward = onward_ref[...] + came_ref[:, quarter:].astype(jnp.float32)
    onward_out[...] = onward.astype(jnp.bfloat16)


def fold(keep, onward, came):
    return pl.pallas_call(
        fold_kernel,
        in_specs=[VMEM] * 3,
        out_specs=[VMEM] * 2,
        out_shape=[
            jax.ShapeDtypeStruct(keep.shape, jnp.float32),
            jax.ShapeDtypeStruct(onward.shape, jnp.bfloat16),
        ],
        compiler_params=pltpu.CompilerParams(vmem_limit_bytes=8 << 20),
        name="fold",
    )(keep, onward, came)


def total_kernel(keep_ref, came_ref, out_ref):
    out_ref[...] = (keep_ref[...] + came_ref[...].astype(jnp.float32)).astype(jnp.bfloat16)


def total_of(keep, came):
    return pl.pallas_call(
        total_kernel,
        in_specs=[VMEM] * 2,
        out_specs=VMEM,
        out_shape=jax.ShapeDtypeStruct(keep.shape, jnp.bfloat16),
        compiler_params=pltpu.CompilerParams(vmem_limit_bytes=8 << 20),
        name="total",
    )(keep, came)


def last_kernel(own_ref, keep_ref, came_ref, home_ref, out_ref):
    total = own_ref[...].astype(jnp.float32) + keep_ref[...]
    total = total + came_ref[...].astype(jnp.float32) + home_ref[...].astype(jnp.float32)
    out_ref[...] = total.astype(jnp.bfloat16)


def last(own, keep, came, home):
    return pl.pallas_call(
        last_kernel,
        in_specs=[VMEM] * 4,
        out_specs=VMEM,
        out_shape=jax.ShapeDtypeStruct(own.shape, jnp.bfloat16),
        compiler_params=pltpu.CompilerParams(vmem_limit_bytes=8 << 20),
        name="last",
    )(own, keep, came, home)


def expert_kernel(slices, x_ref, *refs):
    weights = refs[: 3 * slices]
    out_ref, held, total, sems = refs[3 * slices :]
    block = total.shape[0]
    copies = [
        pltpu.make_async_copy(weights[i], held.at[i], sems.at[i]) for i in range(3 * slices)
    ]
    for copy in copies:
        copy.start()

    def step(i, carry):
        number, j = i // slices, i % slices
        start = pl.multiple_of(number * block, block)

        def arrive(k):
            @pl.when(number == 0)
            def _():
                pltpu.make_async_copy(weights[k], held.at[3 * j + k], sems.at[3 * j + k]).wait()

        x = x_ref[pl.ds(start, block), :]
        arrive(0)
        gate = lax.dot_general(x, held[3 * j], NT, preferred_element_type=jnp.float32)
        arrive(1)
        upper = lax.dot_general(x, held[3 * j + 1], NT, preferred_element_type=jnp.float32)
        act = (gate / (1.0 + jnp.exp(-gate)) * upper).astype(jnp.bfloat16)
        arrive(2)
        part = jnp.dot(act, held[3 * j + 2], preferred_element_type=jnp.float32)

        @pl.when(j == 0)
        def _():
            total[...] = part

        @pl.when((j > 0) & (j < slices - 1))
        def _():
            total[...] += part

        @pl.when(j == slices - 1)
        def _():
            out_ref[pl.ds(start, block), :] = (total[...] + part).astype(jnp.bfloat16)

        return carry

    lax.fori_loop(0, x_ref.shape[0] // block * slices, step, 0)


def expert(inbox, weights):
    rows, width = inbox.shape[0] * inbox.shape[1], inbox.shape[2]
    units = weights[0].shape[0]
    count = len(weights)
    block = min(rows, 256)
    out = pl.pallas_call(
        lambda *refs: expert_kernel(count // 3, *refs),
        in_specs=[VMEM] + [pl.BlockSpec(memory_space=pl.ANY)] * count,
        out_specs=VMEM,
        out_shape=jax.ShapeDtypeStruct((rows, width), jnp.bfloat16),
        scratch_shapes=[
            pltpu.VMEM((count, units, width), jnp.bfloat16),
            pltpu.VMEM((block, width), jnp.float32),
            pltpu.SemaphoreType.DMA((count,)),
        ],
        cost_estimate=pl.CostEstimate(
            flops=2 * count * rows * width * units,
            transcendentals=rows * units * count // 3,
            bytes_accessed=2 * count * units * width + 4 * rows * width,
        ),
        name="expert",
    )(inbox.reshape(rows, width), *weights)
    return out.reshape(inbox.shape)


def stage_kernel(scalars_ref, k_ref, v_ref, ck_ref, cv_ref, *outs):
    me, length = scalars_ref[0], scalars_ref[1]
    block = k_ref.shape[0]
    last = ck_ref.shape[0] // block - 1
    for mask, out_ref in enumerate(outs):
        peer = me ^ mask
        start = pl.multiple_of(jnp.minimum(peer, last) * block, block)
        row = lax.broadcasted_iota(jnp.int32, (block, block), 0) + peer * block - length
        moved = row == lax.broadcasted_iota(jnp.int32, (block, block), 1)
        moved = jnp.where(moved, 1.0, 0.0).astype(jnp.bfloat16)
        for which, (fresh_ref, cached_ref) in enumerate(((k_ref, ck_ref), (v_ref, cv_ref))):
            fresh = jnp.dot(moved, fresh_ref[...], preferred_element_type=jnp.float32)
            kept = cached_ref[pl.ds(start, block), :].astype(jnp.float32)
            old = lax.broadcasted_iota(jnp.int32, kept.shape, 0) + peer * block < length
            out_ref[which] = jnp.where(old, kept, fresh).astype(jnp.bfloat16)


def stage(scalars, span_k, span_v, cache_k, cache_v, pieces):
    span, columns = span_k.shape
    return pl.pallas_call(
        stage_kernel,
        in_specs=[SMEM] + [VMEM] * 4,
        out_specs=[VMEM] * pieces,
        out_shape=[jax.ShapeDtypeStruct((2, span, columns), jnp.bfloat16)] * pieces,
        compiler_params=pltpu.CompilerParams(vmem_limit_bytes=32 << 20),
        name="stage",
    )(scalars, span_k, span_v, cache_k, cache_v)


def join_kernel(scalars_ref, *refs):
    out_ref = refs[-1]
    columns = refs[0].shape[2]
    for mask, ref in enumerate(refs[:-1]):
        out_ref[:, :, lanes((scalars_ref[0] ^ mask) * columns, columns)] = ref[...]


def join(scalars, pieces):
    kinds, block, columns = pieces[0].shape
    return pl.pallas_call(
        join_kernel,
        in_specs=[SMEM] + [VMEM] * len(pieces),
        out_specs=VMEM,
        out_shape=jax.ShapeDtypeStruct((kinds, block, columns * len(pieces)), jnp.bfloat16),
        compiler_params=pltpu.CompilerParams(vmem_limit_bytes=16 << 20),
        name="join",
    )(scalars, *pieces)


def flip(value, mask):
    groups = lax.axis_size("tensor")
    return lax.ppermute(value, "tensor", [(i, i ^ mask) for i in range(groups)])


def along(value, step):
    count = lax.axis_size("request")
    pairs = [(i, i // RING * RING + (i + step) % RING) for i in range(count)]
    return lax.ppermute(value, "request", pairs)


def homeward(value, gap):
    count, groups = lax.axis_size("request"), lax.axis_size("tensor")
    pairs = []
    for i in range(count):
        for t in range(groups):
            to = (i + (gap if t // 2 else -gap)) % RING + i // RING * RING
            pairs.append((t * count + i, (t ^ 2) * count + to))
    return lax.ppermute(value, ("tensor", "request"), pairs)


def on_device(
    hidden_in,
    span_q,
    span_k,
    span_v,
    cache_k,
    cache_v,
    cached_len,
    out_proj,
    norm_gain,
    routes,
    route_weight,
    w_gate,
    w_up,
    w_down,
):
    span, width = hidden_in.shape
    groups = lax.axis_size("tensor")
    experts = lax.axis_size("request")
    plane = experts // RING
    me = lax.axis_index("tensor")
    core = me % 2
    chip = me // 2
    layer = lax.axis_index("request") % RING
    length = cached_len[0]
    planes = [[column * RING + z for column in range(plane)] for z in range(RING)]
    scalars = jnp.stack([chip, core, layer]).astype(jnp.int32)

    def exchange(value):
        return lax.all_to_all(
            value, "request", split_axis=0, concat_axis=0, axis_index_groups=planes, tiled=True
        )

    own_w = (jnp.swapaxes(w_gate[0], 0, 1), jnp.swapaxes(w_up[0], 0, 1), w_down[0])
    near_w = tuple(flip(w, 1) for w in own_w)
    weights = own_w + near_w

    most = max(2, 2 * span * TOP // experts)
    share = most // 2
    table = jnp.concatenate([routes.T.astype(jnp.float32), route_weight.T], axis=0)
    tables = {0: table}
    for step in (1, -1, 2):
        tables[step] = along(table, step)

    keep, send = attend(
        jnp.stack([length, core]).astype(jnp.int32),
        span_q,
        span_k,
        span_v,
        cache_k[0],
        cache_v[0],
        out_proj,
        1,
    )
    keep = keep + flip(send, 1).astype(jnp.float32)
    came = flip(keep.astype(jnp.bfloat16), 2)
    mixed_half = mixed_of(scalars, 0, hidden_in, keep, came)
    mine, other, own_mixed = norm(
        scalars, mixed_half, flip(mixed_half, 1), norm_gain.reshape(1, width)
    )

    tokens = {0: (mine, other)}
    for step in (1, -1, 2):
        came = along(mine, step)
        tokens[step] = (came, flip(came, 1))

    chunks = ((0,), (1, -1), (2,))
    outs = []
    for steps in chunks:
        outbox = dispatch(scalars, plane, share, [(tables[step],) + tokens[step] for step in steps])
        inbox = exchange(outbox)
        outs.append(expert(inbox, weights))

    def gather(kind, number, steps):
        returned = exchange(outs[number])
        keep, onward, send = combine(
            kind, scalars, plane, share, [tables[step] for step in steps], returned
        )
        return keep, onward, flip(send, 1)

    homes = []
    for kind, number, gap in (("pair", 1, 1), ("far", 2, 2)):
        keep, onward, came = gather(kind, number, chunks[number])
        keep, onward = fold(keep, onward, came)
        came = flip(onward, 2)
        keep = total_of(keep, came)
        homes.append(homeward(keep, gap))
    keep, onward, came = gather("own", 0, chunks[0])
    keep, onward = close(scalars, keep, onward, came, homes[0])
    came = flip(onward, 2)
    layer_out = last(own_mixed, keep, came, homes[1])

    spot = jnp.stack([me, length]).astype(jnp.int32)
    pieces = stage(spot, span_k, span_v, cache_k[0], cache_v[0], groups)
    pieces = [pieces[0]] + [flip(pieces[m], m) for m in range(1, groups)]
    decode = join(spot, pieces)
    return (layer_out, decode[None])


def solution(mesh):
    in_specs = (
        P("request", None),
        P("request", "tensor"),
        P("request", "tensor"),
        P("request", "tensor"),
        P("request", None, "tensor"),
        P("request", None, "tensor"),
        P("request"),
        P("tensor", None),
        P(),
        P("request", None),
        P("request", None),
        P("request", None, "tensor"),
        P("request", None, "tensor"),
        P("request", "tensor", None),
    )
    out_specs = (P("request", "tensor"), P("request", None, "tensor", None))

    return jax.shard_map(
        on_device, mesh=mesh, in_specs=in_specs, out_specs=out_specs, check_vma=False
    )
```

```python
import jax
import jax.numpy as jnp
from jax import lax
from jax.experimental import pallas as pl
from jax.experimental.pallas import tpu as pltpu
from jax.sharding import PartitionSpec as P


HD = 128
TOP = 4
RING = 4


eps = 1e-06
neg_large = -1e30


NT = (((1,), (1,)), ((), ()))
TN = (((0,), (0,)), ((), ()))
VMEM = pl.BlockSpec(memory_space=pltpu.VMEM)
SMEM = pl.BlockSpec(memory_space=pltpu.SMEM)


def lanes(start, size):
    return pl.ds(pl.multiple_of(start, 128), size)


def attend_kernel(scalars_ref, q_ref, k_ref, v_ref, ck_ref, cv_ref, w_ref, *refs):
    outs, part_ref = refs[:-1], refs[-1]
    group = pl.program_id(0)
    length, core = scalars_ref[0], scalars_ref[1]
    scale = HD ** (-0.5)
    attended = []
    for head in range(q_ref.shape[1] // HD):
        own = slice(head * HD, (head + 1) * HD)
        query = q_ref[:, own]
        old = lax.dot_general(query, ck_ref[:, own], NT, preferred_element_type=jnp.float32) * scale
        new = lax.dot_general(query, k_ref[:, own], NT, preferred_element_type=jnp.float32) * scale
        old = jnp.where(lax.broadcasted_iota(jnp.int32, old.shape, 1) < length, old, neg_large)
        rows = lax.broadcasted_iota(jnp.int32, new.shape, 0)
        new = jnp.where(lax.broadcasted_iota(jnp.int32, new.shape, 1) <= rows, new, neg_large)
        top = jnp.maximum(
            jnp.max(old, axis=1, keepdims=True), jnp.max(new, axis=1, keepdims=True)
        )
        old = jnp.exp(old - top)
        new = jnp.exp(new - top)
        total = jnp.sum(old, axis=1, keepdims=True) + jnp.sum(new, axis=1, keepdims=True)
        inverse = 1.0 / total
        result = jnp.dot(
            (old * inverse).astype(jnp.bfloat16), cv_ref[:, own], preferred_element_type=jnp.float32
        ) + jnp.dot(
            (new * inverse).astype(jnp.bfloat16), v_ref[:, own], preferred_element_type=jnp.float32
        )
        attended.append(result.astype(jnp.bfloat16))
    part = jnp.dot(
        jnp.concatenate(attended, axis=1), w_ref[...], preferred_element_type=jnp.float32
    )

    @pl.when(group == 0)
    def _():
        part_ref[...] = part

    @pl.when(group > 0)
    def _():
        part_ref[...] += part

    @pl.when(group == pl.num_programs(0) - 1)
    def _():
        rows, half = outs[0].shape
        for i in range(len(outs) // 2):
            keep_ref, send_ref = outs[2 * i : 2 * i + 2]
            own = slice(i * rows, (i + 1) * rows)
            keep_ref[...] = part_ref[own, lanes(core * half, half)]
            send_ref[...] = part_ref[own, lanes((1 - core) * half, half)].astype(jnp.bfloat16)


def attend(scalars, span_q, span_k, span_v, cache_k, cache_v, out_proj, pieces):
    span, columns = span_q.shape
    prior = cache_k.shape[0]
    width = out_proj.shape[1]
    heads = columns // HD
    wide = 2 * HD if heads % 2 == 0 else HD
    rows = span // pieces
    fresh = pl.BlockSpec((span, wide), lambda h, n: (0, h))
    cached = pl.BlockSpec((prior, wide), lambda h, n: (0, h))
    halves = pl.BlockSpec((rows, width // 2), lambda h, n: (0, 0))
    out = [
        jax.ShapeDtypeStruct((rows, width // 2), jnp.float32),
        jax.ShapeDtypeStruct((rows, width // 2), jnp.bfloat16),
    ]
    return pl.pallas_call(
        attend_kernel,
        grid_spec=pltpu.PrefetchScalarGridSpec(
            num_scalar_prefetch=1,
            grid=(columns // wide,),
            in_specs=[
                fresh,
                fresh,
                fresh,
                cached,
                cached,
                pl.BlockSpec((wide, width), lambda h, n: (h, 0)),
            ],
            out_specs=[halves] * (2 * pieces),
            scratch_shapes=[pltpu.VMEM((span, width), jnp.float32)],
        ),
        out_shape=out * pieces,
        cost_estimate=pl.CostEstimate(
            flops=heads * span * (4 * (prior + span) * HD + 2 * HD * width),
            transcendentals=heads * span * (prior + span),
            bytes_accessed=9 << 20,
        ),
        name="attend",
    )(scalars, span_q, span_k, span_v, cache_k, cache_v, out_proj)


def mixed_kernel(scalars_ref, hidden_ref, part_ref, came_ref, out_ref):
    total = hidden_ref[...].astype(jnp.float32) + part_ref[...]
    out_ref[...] = (total + came_ref[...].astype(jnp.float32)).astype(jnp.bfloat16)


def mixed_of(scalars, piece, hidden, part, came):
    rows, half = part.shape
    whole = pl.BlockSpec((rows, half), lambda i, n: (0, 0))
    return pl.pallas_call(
        mixed_kernel,
        grid_spec=pltpu.PrefetchScalarGridSpec(
            num_scalar_prefetch=1,
            grid=(1,),
            in_specs=[pl.BlockSpec((rows, half), lambda i, n: (piece, n[1])), whole, whole],
            out_specs=whole,
        ),
        out_shape=jax.ShapeDtypeStruct((rows, half), jnp.bfloat16),
        compiler_params=pltpu.CompilerParams(vmem_limit_bytes=8 << 20),
        name="mixed",
    )(scalars, hidden, part, came)


def norm_kernel(scalars_ref, mine_ref, other_ref, gain_ref, mine_out, other_out, own_out):
    chip, core = scalars_ref[0], scalars_ref[1]
    half = mine_ref.shape[1]
    quarter = half // 2
    mine = mine_ref[...].astype(jnp.float32)
    other = other_ref[...].astype(jnp.float32)
    total = jnp.sum(mine * mine, axis=1, keepdims=True) + jnp.sum(
        other * other, axis=1, keepdims=True
    )
    scale = lax.rsqrt(total / (2 * half) + eps)
    mine_gain = gain_ref[:, lanes(core * half, half)]
    other_gain = gain_ref[:, lanes((1 - core) * half, half)]
    mine_out[...] = (mine * scale * mine_gain).astype(jnp.bfloat16)
    other_out[...] = (other * scale * other_gain).astype(jnp.bfloat16)

    @pl.when(chip == core)
    def _():
        own_out[...] = mine_ref[:, lanes(core * quarter, quarter)]

    @pl.when(chip != core)
    def _():
        own_out[...] = other_ref[:, lanes(core * quarter, quarter)]


def norm(scalars, mine, other, gain):
    span, half = mine.shape
    return pl.pallas_call(
        norm_kernel,
        in_specs=[SMEM, VMEM, VMEM, VMEM],
        out_specs=[VMEM] * 3,
        out_shape=[
            jax.ShapeDtypeStruct((span, half), jnp.bfloat16),
            jax.ShapeDtypeStruct((span, half), jnp.bfloat16),
            jax.ShapeDtypeStruct((span, half // 2), jnp.bfloat16),
        ],
        compiler_params=pltpu.CompilerParams(vmem_limit_bytes=16 << 20),
        name="norm",
    )(scalars, mine, other, gain)


def slots(scalars_ref, table_ref, plane, share):
    core, layer = scalars_ref[1], scalars_ref[2]
    span = table_ref.shape[1]
    ids = lax.broadcasted_iota(jnp.int32, (plane, span), 0) * RING + layer
    ids = ids.astype(jnp.float32)
    member = jnp.zeros((plane, span), jnp.float32)
    weight = jnp.zeros((plane, span), jnp.float32)
    for k in range(TOP):
        hit = table_ref[k : k + 1, :] == ids
        member = jnp.where(hit, 1.0, member)
        weight = jnp.where(hit, table_ref[TOP + k : TOP + k + 1, :], weight)
    earlier = lax.broadcasted_iota(jnp.int32, (span, span), 0) < lax.broadcasted_iota(
        jnp.int32, (span, span), 1
    )
    rank = jnp.dot(
        member.astype(jnp.bfloat16),
        earlier.astype(jnp.float32).astype(jnp.bfloat16),
        preferred_element_type=jnp.float32,
    )
    slot = jnp.where(member > 0.0, rank - (core * share).astype(jnp.float32), -1.0)
    shape = (plane, share, span)
    wanted = lax.broadcasted_iota(jnp.int32, shape, 1).astype(jnp.float32)
    chosen = jnp.broadcast_to(slot[:, None, :], shape) == wanted
    return chosen, weight


def dispatch_kernel(plane, share, scalars_ref, *refs):
    count = (len(refs) - 1) // 3
    out_ref = refs[-1]
    core = scalars_ref[1]
    for r in range(count):
        table_ref, mine_ref, other_ref = refs[3 * r : 3 * r + 3]
        half = mine_ref.shape[1]
        chosen, _ = slots(scalars_ref, table_ref, plane, share)
        select = jnp.where(chosen, 1.0, 0.0).reshape(plane * share, chosen.shape[2])
        select = select.astype(jnp.bfloat16)
        for ref, which in ((mine_ref, core), (other_ref, 1 - core)):
            rows = jnp.dot(select, ref[...], preferred_element_type=jnp.float32)
            rows = rows.astype(jnp.bfloat16).reshape(plane, share, half)
            out_ref[:, r * share : (r + 1) * share, lanes(which * half, half)] = rows


def dispatch(scalars, plane, share, items):
    count = len(items)
    half = items[0][1].shape[1]
    return pl.pallas_call(
        lambda *refs: dispatch_kernel(plane, share, *refs),
        in_specs=[SMEM] + [VMEM] * (3 * count),
        out_specs=VMEM,
        out_shape=jax.ShapeDtypeStruct((plane, count * share, 2 * half), jnp.bfloat16),
        compiler_params=pltpu.CompilerParams(vmem_limit_bytes=24 << 20),
        name="dispatch",
    )(scalars, *[part for item in items for part in item])


def combine_kernel(kind, count, plane, share, scalars_ref, *refs):
    tables, rows_ref = refs[:count], refs[count]
    keep_ref, pass_ref, send_ref = refs[count + 1 :]
    chip, core = scalars_ref[0], scalars_ref[1]
    quarter = rows_ref.shape[2] // 4

    def mixer(table, r):
        chosen, weight = slots(scalars_ref, table, plane, share)
        high = weight.astype(jnp.bfloat16).astype(jnp.float32)
        mixes = []
        for w in (high, weight - high):
            mix = jnp.where(chosen, jnp.broadcast_to(w[:, None, :], chosen.shape), 0.0)
            mixes.append(mix.reshape(plane * share, chosen.shape[2]).astype(jnp.bfloat16))

        def mixture(its_chip, its_core):
            start = pl.multiple_of(r * share, share)
            columns = lanes((2 * its_chip + its_core) * quarter, quarter)
            rows = rows_ref[:, pl.ds(start, share), columns].reshape(plane * share, quarter)
            return sum(
                lax.dot_general(mix, rows, TN, preferred_element_type=jnp.float32) for mix in mixes
            )

        return mixture

    if kind == "pair":
        down, up = tables[0][...], tables[1][...]
        here = jnp.where(chip == 1, 1, 0)
        keeper = mixer(jnp.where(chip == 1, up, down), here)
        passer = mixer(jnp.where(chip == 1, down, up), 1 - here)
        parts = [(keeper, 0), (keeper, 1), (passer, 0), (passer, 1)]
    else:
        only = mixer(tables[0][...], 0)
        parts = [(only, chip), (only, 1 - chip)] if kind == "own" else [(only, 1 - chip), (only, chip)]
    each = len(parts) // 2
    for i, (mixture, its_chip) in enumerate(parts):
        out_ref = keep_ref if i < each else pass_ref
        place = i % each * quarter
        out_ref[:, place : place + quarter] = mixture(its_chip, core)
        sent = mixture(its_chip, 1 - core)
        send_ref[:, i * quarter : (i + 1) * quarter] = sent.astype(jnp.bfloat16)


def combine(kind, scalars, plane, share, tables, rows):
    span = tables[0].shape[1]
    width = rows.shape[2] // 4 * (2 if kind == "pair" else 1)
    count = len(tables)
    return pl.pallas_call(
        lambda *refs: combine_kernel(kind, count, plane, share, *refs),
        in_specs=[SMEM] + [VMEM] * (count + 1),
        out_specs=[VMEM] * 3,
        out_shape=[
            jax.ShapeDtypeStruct((span, width), jnp.float32),
            jax.ShapeDtypeStruct((span, width), jnp.float32),
            jax.ShapeDtypeStruct((span, 2 * width), jnp.bfloat16),
        ],
        compiler_params=pltpu.CompilerParams(vmem_limit_bytes=24 << 20),
        name="combine",
    )(scalars, *tables, rows)


def close_kernel(scalars_ref, keep_ref, onward_ref, came_ref, home_ref, keep_out, onward_out):
    chip = scalars_ref[0]
    quarter = keep_ref.shape[1]
    mine = home_ref[:, lanes(chip * quarter, quarter)].astype(jnp.float32)
    other = home_ref[:, lanes((1 - chip) * quarter, quarter)].astype(jnp.float32)
    keep_out[...] = keep_ref[...] + came_ref[:, :quarter].astype(jnp.float32) + mine
    onward = onward_ref[...] + came_ref[:, quarter:].astype(jnp.float32) + other
    onward_out[...] = onward.astype(jnp.bfloat16)


def close(scalars, keep, onward, came, home):
    return pl.pallas_call(
        close_kernel,
        in_specs=[SMEM] + [VMEM] * 4,
        out_specs=[VMEM] * 2,
        out_shape=[
            jax.ShapeDtypeStruct(keep.shape, jnp.float32),
            jax.ShapeDtypeStruct(onward.shape, jnp.bfloat16),
        ],
        compiler_params=pltpu.CompilerParams(vmem_limit_bytes=8 << 20),
        name="close",
    )(scalars, keep, onward, came, home)


def fold_kernel(keep_ref, onward_ref, came_ref, keep_out, onward_out):
    quarter = keep_ref.shape[1]
    keep_out[...] = keep_ref[...] + came_ref[:, :quarter].astype(jnp.float32)
    onward = onward_ref[...] + came_ref[:, quarter:].astype(jnp.float32)
    onward_out[...] = onward.astype(jnp.bfloat16)


def fold(keep, onward, came):
    return pl.pallas_call(
        fold_kernel,
        in_specs=[VMEM] * 3,
        out_specs=[VMEM] * 2,
        out_shape=[
            jax.ShapeDtypeStruct(keep.shape, jnp.float32),
            jax.ShapeDtypeStruct(onward.shape, jnp.bfloat16),
        ],
        compiler_params=pltpu.CompilerParams(vmem_limit_bytes=8 << 20),
        name="fold",
    )(keep, onward, came)


def sum_kernel(keep_ref, came_ref, keep_out, send_out):
    total = keep_ref[...] + came_ref[...].astype(jnp.float32)
    keep_out[...] = total
    send_out[...] = total.astype(jnp.bfloat16)


def sum_of(keep, came):
    return pl.pallas_call(
        sum_kernel,
        in_specs=[VMEM] * 2,
        out_specs=[VMEM] * 2,
        out_shape=[
            jax.ShapeDtypeStruct(keep.shape, jnp.float32),
            jax.ShapeDtypeStruct(keep.shape, jnp.bfloat16),
        ],
        compiler_params=pltpu.CompilerParams(vmem_limit_bytes=8 << 20),
        name="sum",
    )(keep, came)


def total_kernel(keep_ref, came_ref, out_ref):
    out_ref[...] = (keep_ref[...] + came_ref[...].astype(jnp.float32)).astype(jnp.bfloat16)


def total_of(keep, came):
    return pl.pallas_call(
        total_kernel,
        in_specs=[VMEM] * 2,
        out_specs=VMEM,
        out_shape=jax.ShapeDtypeStruct(keep.shape, jnp.bfloat16),
        compiler_params=pltpu.CompilerParams(vmem_limit_bytes=8 << 20),
        name="total",
    )(keep, came)


def last_kernel(own_ref, keep_ref, came_ref, home_ref, out_ref):
    total = own_ref[...].astype(jnp.float32) + keep_ref[...]
    total = total + came_ref[...].astype(jnp.float32) + home_ref[...].astype(jnp.float32)
    out_ref[...] = total.astype(jnp.bfloat16)


def last(own, keep, came, home):
    return pl.pallas_call(
        last_kernel,
        in_specs=[VMEM] * 4,
        out_specs=VMEM,
        out_shape=jax.ShapeDtypeStruct(own.shape, jnp.bfloat16),
        compiler_params=pltpu.CompilerParams(vmem_limit_bytes=8 << 20),
        name="last",
    )(own, keep, came, home)


def expert_kernel(slices, x_ref, *refs):
    weights = refs[: 3 * slices]
    out_ref, held, total, sems = refs[3 * slices :]
    block = total.shape[0]
    copies = [
        pltpu.make_async_copy(weights[i], held.at[i], sems.at[i]) for i in range(3 * slices)
    ]
    for copy in copies:
        copy.start()

    def step(i, carry):
        number, j = i // slices, i % slices
        start = pl.multiple_of(number * block, block)

        def arrive(k):
            @pl.when(number == 0)
            def _():
                pltpu.make_async_copy(weights[k], held.at[3 * j + k], sems.at[3 * j + k]).wait()

        x = x_ref[pl.ds(start, block), :]
        arrive(0)
        gate = lax.dot_general(x, held[3 * j], NT, preferred_element_type=jnp.float32)
        arrive(1)
        upper = lax.dot_general(x, held[3 * j + 1], NT, preferred_element_type=jnp.float32)
        act = (gate / (1.0 + jnp.exp(-gate)) * upper).astype(jnp.bfloat16)
        arrive(2)
        part = jnp.dot(act, held[3 * j + 2], preferred_element_type=jnp.float32)

        @pl.when(j == 0)
        def _():
            total[...] = part

        @pl.when((j > 0) & (j < slices - 1))
        def _():
            total[...] += part

        @pl.when(j == slices - 1)
        def _():
            out_ref[pl.ds(start, block), :] = (total[...] + part).astype(jnp.bfloat16)

        return carry

    lax.fori_loop(0, x_ref.shape[0] // block * slices, step, 0)


def expert(inbox, weights):
    rows, width = inbox.shape[0] * inbox.shape[1], inbox.shape[2]
    units = weights[0].shape[0]
    count = len(weights)
    block = min(rows, 256)
    out = pl.pallas_call(
        lambda *refs: expert_kernel(count // 3, *refs),
        in_specs=[VMEM] + [pl.BlockSpec(memory_space=pl.ANY)] * count,
        out_specs=VMEM,
        out_shape=jax.ShapeDtypeStruct((rows, width), jnp.bfloat16),
        scratch_shapes=[
            pltpu.VMEM((count, units, width), jnp.bfloat16),
            pltpu.VMEM((block, width), jnp.float32),
            pltpu.SemaphoreType.DMA((count,)),
        ],
        cost_estimate=pl.CostEstimate(
            flops=2 * count * rows * width * units,
            transcendentals=rows * units * count // 3,
            bytes_accessed=2 * count * units * width + 4 * rows * width,
        ),
        name="expert",
    )(inbox.reshape(rows, width), *weights)
    return out.reshape(inbox.shape)


def stage_kernel(scalars_ref, k_ref, v_ref, ck_ref, cv_ref, *outs):
    me, length = scalars_ref[0], scalars_ref[1]
    block = k_ref.shape[0]
    last = ck_ref.shape[0] // block - 1
    for mask, out_ref in enumerate(outs):
        peer = me ^ mask
        start = pl.multiple_of(jnp.minimum(peer, last) * block, block)
        row = lax.broadcasted_iota(jnp.int32, (block, block), 0) + peer * block - length
        moved = row == lax.broadcasted_iota(jnp.int32, (block, block), 1)
        moved = jnp.where(moved, 1.0, 0.0).astype(jnp.bfloat16)
        for which, (fresh_ref, cached_ref) in enumerate(((k_ref, ck_ref), (v_ref, cv_ref))):
            fresh = jnp.dot(moved, fresh_ref[...], preferred_element_type=jnp.float32)
            kept = cached_ref[pl.ds(start, block), :].astype(jnp.float32)
            old = lax.broadcasted_iota(jnp.int32, kept.shape, 0) + peer * block < length
            out_ref[which] = jnp.where(old, kept, fresh).astype(jnp.bfloat16)


def stage(scalars, span_k, span_v, cache_k, cache_v, pieces):
    span, columns = span_k.shape
    return pl.pallas_call(
        stage_kernel,
        in_specs=[SMEM] + [VMEM] * 4,
        out_specs=[VMEM] * pieces,
        out_shape=[jax.ShapeDtypeStruct((2, span, columns), jnp.bfloat16)] * pieces,
        compiler_params=pltpu.CompilerParams(vmem_limit_bytes=32 << 20),
        name="stage",
    )(scalars, span_k, span_v, cache_k, cache_v)


def join_kernel(scalars_ref, *refs):
    out_ref = refs[-1]
    columns = refs[0].shape[2]
    for mask, ref in enumerate(refs[:-1]):
        out_ref[:, :, lanes((scalars_ref[0] ^ mask) * columns, columns)] = ref[...]


def join(scalars, pieces):
    kinds, block, columns = pieces[0].shape
    return pl.pallas_call(
        join_kernel,
        in_specs=[SMEM] + [VMEM] * len(pieces),
        out_specs=VMEM,
        out_shape=jax.ShapeDtypeStruct((kinds, block, columns * len(pieces)), jnp.bfloat16),
        compiler_params=pltpu.CompilerParams(vmem_limit_bytes=16 << 20),
        name="join",
    )(scalars, *pieces)


def flip(value, mask):
    groups = lax.axis_size("tensor")
    return lax.ppermute(value, "tensor", [(i, i ^ mask) for i in range(groups)])


def along(value, step):
    count = lax.axis_size("request")
    pairs = [(i, i // RING * RING + (i + step) % RING) for i in range(count)]
    return lax.ppermute(value, "request", pairs)


def homeward(value, gap):
    count, groups = lax.axis_size("request"), lax.axis_size("tensor")
    pairs = []
    for i in range(count):
        for t in range(groups):
            to = (i + (gap if t // 2 else -gap)) % RING + i // RING * RING
            pairs.append((t * count + i, (t ^ 2) * count + to))
    return lax.ppermute(value, ("tensor", "request"), pairs)


def on_device(
    hidden_in,
    span_q,
    span_k,
    span_v,
    cache_k,
    cache_v,
    cached_len,
    out_proj,
    norm_gain,
    routes,
    route_weight,
    w_gate,
    w_up,
    w_down,
):
    span, width = hidden_in.shape
    groups = lax.axis_size("tensor")
    experts = lax.axis_size("request")
    plane = experts // RING
    me = lax.axis_index("tensor")
    core = me % 2
    chip = me // 2
    layer = lax.axis_index("request") % RING
    length = cached_len[0]
    planes = [[column * RING + z for column in range(plane)] for z in range(RING)]
    scalars = jnp.stack([chip, core, layer]).astype(jnp.int32)

    def exchange(value):
        return lax.all_to_all(
            value, "request", split_axis=0, concat_axis=0, axis_index_groups=planes, tiled=True
        )

    own_w = (jnp.swapaxes(w_gate[0], 0, 1), jnp.swapaxes(w_up[0], 0, 1), w_down[0])
    near_w = tuple(flip(w, 1) for w in own_w)
    weights = own_w + near_w

    most = max(2, 2 * span * TOP // experts)
    share = most // 2
    table = jnp.concatenate([routes.T.astype(jnp.float32), route_weight.T], axis=0)
    tables = {0: table}
    for step in (1, -1, 2):
        tables[step] = along(table, step)

    keep, send = attend(
        jnp.stack([length, core]).astype(jnp.int32),
        span_q,
        span_k,
        span_v,
        cache_k[0],
        cache_v[0],
        out_proj,
        1,
    )
    keep, send = sum_of(keep, flip(send, 1))
    came = flip(send, 2)
    mixed_half = mixed_of(scalars, 0, hidden_in, keep, came)
    mine, other, own_mixed = norm(
        scalars, mixed_half, flip(mixed_half, 1), norm_gain.reshape(1, width)
    )

    tokens = {0: (mine, other)}
    for step in (1, -1, 2):
        came = along(mine, step)
        tokens[step] = (came, flip(came, 1))

    chunks = ((0,), (1, -1), (2,))
    outs = []
    for steps in chunks:
        outbox = dispatch(scalars, plane, share, [(tables[step],) + tokens[step] for step in steps])
        inbox = exchange(outbox)
        outs.append(expert(inbox, weights))

    def gather(kind, number, steps):
        returned = exchange(outs[number])
        keep, onward, send = combine(
            kind, scalars, plane, share, [tables[step] for step in steps], returned
        )
        return keep, onward, flip(send, 1)

    homes = []
    for kind, number, gap in (("pair", 1, 1), ("far", 2, 2)):
        keep, onward, came = gather(kind, number, chunks[number])
        keep, onward = fold(keep, onward, came)
        came = flip(onward, 2)
        keep = total_of(keep, came)
        homes.append(homeward(keep, gap))
    keep, onward, came = gather("own", 0, chunks[0])
    keep, onward = close(scalars, keep, onward, came, homes[0])
    came = flip(onward, 2)
    layer_out = last(own_mixed, keep, came, homes[1])

    spot = jnp.stack([me, length]).astype(jnp.int32)
    pieces = stage(spot, span_k, span_v, cache_k[0], cache_v[0], groups)
    pieces = [pieces[0]] + [flip(pieces[m], m) for m in range(1, groups)]
    decode = join(spot, pieces)
    return (layer_out, decode[None])


def solution(mesh):
    in_specs = (
        P("request", None),
        P("request", "tensor"),
        P("request", "tensor"),
        P("request", "tensor"),
        P("request", None, "tensor"),
        P("request", None, "tensor"),
        P("request"),
        P("tensor", None),
        P(),
        P("request", None),
        P("request", None),
        P("request", None, "tensor"),
        P("request", None, "tensor"),
        P("request", "tensor", None),
    )
    out_specs = (P("request", "tensor"), P("request", None, "tensor", None))

    return jax.shard_map(
        on_device, mesh=mesh, in_specs=in_specs, out_specs=out_specs, check_vma=False
    )
```
